32 devices in a mesh: dp: 8 (over z, x), tensor: 4 (over y, core).
Axes of the slice: x: 2, y: 2, z: 4, core: 2. Of those that a mesh axis runs over, the one named last changes fastest.
Arguments:
- seg_input: bfloat16 [8192, 768], P('dp'), may hold values from -6 to 6
- w_qkv: bfloat16 [768, 3, 768], P(None, None, 'tensor'), may hold values from -0.21875 to 0.21875
- b_qv: bfloat16 [2, 768], P(None, 'tensor'), may hold values from -3 to 3
- w_out: bfloat16 [768, 768], P('tensor'), may hold values from -1.75 to 1.75
- b_out: bfloat16 [768], replicated, may hold values from -2 to 2
- norm1_gain: bfloat16 [768], replicated, may hold values from 0.5 to 1.5
- norm1_bias: bfloat16 [768], replicated, may hold values from -2 to 2
- w_up: bfloat16 [768, 3072], P(None, 'tensor'), may hold values from -0.21875 to 0.21875
- b_up: bfloat16 [3072], P('tensor'), may hold values from -3 to 3
- w_down: bfloat16 [3072, 768], P('tensor'), may hold values from -0.21875 to 0.21875
- b_down: bfloat16 [768], replicated, may hold values from -2 to 2
- norm2_gain: bfloat16 [768], replicated, may hold values from 0.5 to 1.5
- norm2_bias: bfloat16 [768], replicated, may hold values from -2 to 2
- doc_ids: int32 [16, 492], P('dp'), may hold values from 0 to 19, never falling along the last dimension, each value on 1 to 369 neighbouring positions
- mem_live: int32 [16], P('dp'), may hold values from 1 to 10
- out_grad: bfloat16 [8192, 768], P('dp'), may hold values from -6 to 6
Outputs:
- seg_output: bfloat16 [8192, 768], P('dp')
- grad_input: bfloat16 [8192, 768], P('dp')
- grad_w_qkv: float32 [768, 3, 768], P(None, None, 'tensor')
- grad_b_qv: float32 [2, 768], P(None, 'tensor')
- grad_w_out: float32 [768, 768], P('tensor')
- grad_b_out: float32 [768], replicated
- grad_norm1_gain: float32 [768], replicated
- grad_norm1_bias: float32 [768], replicated
- grad_w_up: float32 [768, 3072], P(None, 'tensor')
- grad_b_up: float32 [3072], P('tensor')
- grad_w_down: float32 [3072, 768], P('tensor')
- grad_b_down: float32 [768], replicated
- grad_norm2_gain: float32 [768], replicated
- grad_norm2_bias: float32 [768], replicated
The draws below stay inside these ranges and needn't reach their ends.
Inputs may be any that keep to these rules, and one draw needn't show every extreme that they name: `doc_ids`: a segment's document numbers never fall from one token row to the next. The first mem_live read-memory slots of a segment are live.
All inputs are finite; a program needn't handle non-finite values.
Results may differ from the reference program's by a relative error of at most 0.024.
Values may be sent and summed in bfloat16 or wider, within the bound.
No kernel may reach another device: no remote copies, remote signals or barrier semaphores. Data moves between devices by JAX's collectives and lax.ppermute only.
A program may use at most 128 MiB of HBM per device.

```python
import math
import jax
import jax.numpy as jnp
import numpy as np
from jax import lax

D = 768
HEADS = 12
HEAD = 64
FF = 3072
MEM = 10
SEGTOK = 492
SEG_DEV = 2
SEG = 512
NSEGS = 16
ROWS = 8192
N_DP = 8
N_TENSOR = 4


def with_ends(drawn, rng, least, top_value):
    dims = drawn.shape
    spot = [jax.random.randint(jax.random.fold_in(rng, axis), (), 0, dims[axis]) for axis in range(len(dims))]
    drawn = drawn.at[tuple(spot)].set(least)
    longest = dims.index(max(dims))
    spot[longest] = (spot[longest] + 1) % dims[longest]
    return drawn.at[tuple(spot)].set(top_value)


def shard_levels(stream_key, shape, cuts, low, top_value):
    level = 1.0
    for axis_at, shards_of in cuts:
        heights = jax.random.uniform(jax.random.fold_in(jax.random.fold_in(stream_key, 6), axis_at), (shards_of,), jnp.float32, low / len(cuts), top_value / len(cuts))
        level = level * jnp.repeat(jnp.exp(heights), shape[axis_at] // shards_of).reshape((-1,) + (1,) * (len(shape) - 1 - axis_at))
    return level


def profile(number_of, total, reach, skew):
    loads = [(1 << 20) // math.isqrt(standing ** skew) + 1 for standing in range(2, number_of + 1)]
    spare, holding = total - reach - (number_of - 1), [1] * (number_of - 1)
    while spare > 0:
        candidates = [i for i in range(number_of - 1) if holding[i] < reach]
        whole, remaining = sum([loads[i] for i in candidates]), spare
        for i in candidates:
            extra = min(reach - holding[i], max(1, remaining * loads[i] // whole), spare)
            holding[i] = holding[i] + extra
            spare = spare - extra
    return np.array([reach] + holding)


def ragged(key, amount, total, most, skew):
    if amount == 2:
        one = jax.random.randint(key, (), max(1, total - most), min(most, total - 1) + 1)
        return jnp.stack([one, total - one])
    tallies = jnp.asarray(profile(amount, total, most, skew), jnp.int32)
    couples = (amount - 1) // 2
    source_of, taker = tallies[1:1 + 2 * couples:2], tallies[2:2 + 2 * couples:2]
    slack = jnp.minimum(source_of - 1, most - taker)
    passed = jax.random.randint(jax.random.fold_in(key, 1), (couples,), 0, 1 << 20) % (slack + 1)
    tallies = tallies.at[1:1 + 2 * couples:2].set(source_of - passed).at[2:2 + 2 * couples:2].set(taker + passed)
    return tallies[jax.random.permutation(jax.random.fold_in(key, 2), amount)]


def bell_draw(rng, dims, width, most, cuts=(), kind=jnp.bfloat16):
    gain = shard_levels(rng, dims, cuts, -0.22, 0.18) if cuts else 1.0
    array = jax.random.normal(rng, dims, jnp.float32) * width * gain
    return jnp.minimum(jnp.maximum(array, -most), most).astype(kind)


def setup_inputs(seed: int = 0) -> dict:
    seeds = jax.random.split(jax.random.key(seed), 17)
    return {
        "seg_input": bell_draw(seeds[0], (ROWS, D), 1.0, 6.0, ((0, 8),)),
        "w_qkv": bell_draw(seeds[1], (D, 3, D), D ** -0.5, 0.21875, ((2, 4),)),
        "b_qv": bell_draw(seeds[2], (2, D), 0.5, 3.0, ((1, 4),)),
        "w_out": bell_draw(seeds[3], (D, D), (D // 64) ** -0.5, 1.75, ((0, 4),)),
        "b_out": bell_draw(seeds[4], (D,), 0.3, 2.0),
        "norm1_gain": jnp.clip(1.0 + 0.1 * jax.random.normal(seeds[5], (D,), jnp.float32), 0.5, 1.5).astype(jnp.bfloat16),
        "norm1_bias": bell_draw(seeds[6], (D,), 0.3, 2.0),
        "w_up": bell_draw(seeds[7], (D, FF), D ** -0.5, 0.21875, ((1, 4),)),
        "b_up": bell_draw(seeds[8], (FF,), 0.5, 3.0, ((0, 4),)),
        "w_down": bell_draw(seeds[9], (FF, D), (FF // 4) ** -0.5, 0.21875, ((0, 4),)),
        "b_down": bell_draw(seeds[10], (D,), 0.3, 2.0),
        "norm2_gain": jnp.clip(1.0 + 0.1 * jax.random.normal(seeds[11], (D,), jnp.float32), 0.5, 1.5).astype(jnp.bfloat16),
        "norm2_bias": bell_draw(seeds[12], (D,), 0.3, 2.0),
        "doc_ids": jax.vmap(lambda own: jnp.searchsorted(jnp.cumsum(ragged(own, max(3, SEGTOK // 24), SEGTOK, SEGTOK * 3 // 4, 2)), jnp.arange(SEGTOK), side="right"))(jax.random.split(seeds[13], NSEGS)).reshape((NSEGS, SEGTOK)).astype(jnp.int32),
        "mem_live": with_ends(jax.random.randint(seeds[14], (NSEGS,), 1, MEM + 1), jax.random.fold_in(seeds[14], 1), 1, MEM).astype(jnp.int32),
        "out_grad": bell_draw(seeds[15], (ROWS, D), 1.0, 6.0, ((0, 8),)),
    }


@jax.custom_vjp
def low(v):
    return lax.optimization_barrier(v.astype(jnp.bfloat16)).astype(jnp.float32)

@jax.custom_vjp
def low_back(v):
    return v

def low_keep(v):
    return (low(v), None)

def low_pass(kept, grad):
    return (grad,)

def back_keep(v):
    return (v, None)

def back_low(kept, grad):
    return (low(grad),)
low.defvjp(low_keep, low_pass)
low_back.defvjp(back_keep, back_low)
MASKED_SCORE = -1e+30
NORM_EPS = 1e-05
HIGHEST = lax.Precision.HIGHEST

def matmul(left, right):
    return jnp.dot(left, right, precision=HIGHEST, preferred_element_type=jnp.float32)

def layer_norm(values, norm_gain, norm_shift):
    average = lax.optimization_barrier(jnp.mean(values, axis=-1, keepdims=True))
    centred = values - average
    variance = lax.optimization_barrier(jnp.mean(centred * centred, axis=-1, keepdims=True))
    return centred * lax.rsqrt(variance + NORM_EPS) * norm_gain + norm_shift

def segment_mask(seg_docs, seg_live):
    places = jnp.arange(SEG, dtype=jnp.int32)
    filler = jnp.full((MEM,), -1, jnp.int32)
    tok_doc = jnp.concatenate([filler, seg_docs.astype(jnp.int32), filler])
    is_token = (places >= MEM) & (places < MEM + SEGTOK)
    read_ok = (places < MEM) & (places < seg_live)
    write_ok = places >= MEM + SEGTOK
    token_ok = is_token[None, :] & ((~is_token)[:, None] | (tok_doc[:, None] == tok_doc[None, :]))
    return token_ok | read_ok[None, :] | write_ok[None, :]

def forward(inputs, params, block_docs, block_live):
    w_qkv, b_qv, w_out, b_out, gain_one, shift_one, w_up, b_up, w_down, b_down, gain_two, shift_two = params
    row_data = inputs.reshape(-1, D)
    head_cols = D // N_TENSOR
    unit_cols = FF // N_TENSOR
    score_scale = HEAD ** (-0.5)
    query_parts, key_parts, value_parts = ([], [], [])
    for part_index in range(N_TENSOR):
        columns = slice(part_index * head_cols, (part_index + 1) * head_cols)
        copied = low_back(row_data)
        query_parts.append(low(low_back(matmul(copied, w_qkv[:, 0, columns])) + b_qv[0, columns]))
        key_parts.append(low(low_back(matmul(copied, w_qkv[:, 1, columns]))))
        value_parts.append(low(low_back(matmul(copied, w_qkv[:, 2, columns])) + b_qv[1, columns]))
    shape_four = (-1, SEG, HEADS, HEAD)
    queries = jnp.concatenate(query_parts, axis=1).reshape(shape_four)
    keys_all = jnp.concatenate(key_parts, axis=1).reshape(shape_four)
    values_all = jnp.concatenate(value_parts, axis=1).reshape(shape_four)

    def attend(operands):
        seg_query, seg_key, seg_value, seg_docs, seg_live = operands
        allowed = segment_mask(seg_docs, seg_live)
        scores = low_back(jnp.einsum('qhd,khd->hqk', seg_query, seg_key, precision=HIGHEST) * score_scale)
        scores = jnp.where(allowed[None], scores, MASKED_SCORE)
        soft_weights = jax.nn.softmax(scores, axis=-1)
        return low(low_back(jnp.einsum('hqk,khd->qhd', low(soft_weights), seg_value, precision=HIGHEST)))
    context = lax.map(jax.checkpoint(attend), (queries, keys_all, values_all, block_docs, block_live))
    context = context.reshape(-1, D)
    branch = jnp.zeros_like(row_data)
    for part_index in range(N_TENSOR):
        columns = slice(part_index * head_cols, (part_index + 1) * head_cols)
        branch = branch + low(low_back(matmul(context[:, columns], w_out[columns, :])))
    mixed = row_data + branch + b_out
    normed = layer_norm(mixed, gain_one, shift_one)
    rounded = low(normed)
    down_sum = jnp.zeros_like(row_data)
    for part_index in range(N_TENSOR):
        units = slice(part_index * unit_cols, (part_index + 1) * unit_cols)
        hidden = low_back(matmul(low_back(rounded), w_up[:, units])) + b_up[units]
        activated = low(jax.nn.gelu(hidden, approximate=False))
        down_sum = down_sum + low(low_back(matmul(activated, w_down[units, :])))
    second = normed + down_sum + b_down
    return layer_norm(second, gain_two, shift_two).reshape(inputs.shape)

def reference(seg_input, w_qkv, b_qv, w_out, b_out, norm1_gain, norm1_bias, w_up, b_up, w_down, b_down, norm2_gain, norm2_bias, doc_ids, mem_live, out_grad):
    params = tuple((item.astype(jnp.float32) for item in (w_qkv, b_qv, w_out, b_out, norm1_gain, norm1_bias, w_up, b_up, w_down, b_down, norm2_gain, norm2_bias)))
    total_segs = SEG_DEV * N_DP
    group_size = math.gcd(total_segs, 8)
    group_count = total_segs // group_size
    inputs = seg_input.astype(jnp.float32).reshape(group_count, group_size, SEG, D)
    cotangents = out_grad.astype(jnp.float32).reshape(group_count, group_size, SEG, D)
    group_docs = doc_ids.reshape(group_count, group_size, SEGTOK)
    group_live = mem_live.reshape(group_count, group_size)

    def scan_step(totals, operands):
        block_in, block_docs, block_live, block_cot = operands

        def apply_layer(state_in, param_in):
            return forward(state_in, param_in, block_docs, block_live)
        outputs, pullback = jax.vjp(apply_layer, block_in, params)
        grad_in, grad_params = pullback(block_cot)
        totals = jax.tree.map(lambda left_val, right_val: left_val + right_val, totals, grad_params)
        return (totals, (outputs.astype(jnp.bfloat16), grad_in.astype(jnp.bfloat16)))
    zero_grads = jax.tree.map(jnp.zeros_like, params)
    totals, (outputs, grads) = lax.scan(scan_step, zero_grads, (inputs, group_docs, group_live, cotangents))
    seg_output = outputs.reshape(-1, D)
    grad_input = grads.reshape(-1, D)
    return (seg_output, grad_input, totals[0], totals[1], totals[2], totals[3], totals[4], totals[5], totals[6], totals[7], totals[8], totals[9], totals[10], totals[11])
```

```python
from functools import partial

import jax
import jax.numpy as jnp
from jax import lax
from jax.experimental import pallas as pl
from jax.experimental.pallas import tpu as pltpu
from jax.sharding import PartitionSpec as P

HEAD = 64
MEM = 10
SEGTOK = 492
SEG = 512
HALF = 256
MASKED_SCORE = -1e30
NORM_EPS = 1e-05
BF = jnp.bfloat16
F32 = jnp.float32
B_OUT, GAIN1, SHIFT1, B_DOWN, GAIN2, SHIFT2, B_UP, B_QV = range(8)
V_AT = 256


def dot(left, right, left_dim, right_dim):
    return lax.dot_general(
        left, right, (((left_dim,), (right_dim,)), ((), ())), preferred_element_type=F32
    )


def vmem_call(body, outs, scalars, arrays, flops, scratch=(), trans=0):
    out_shape = [jax.ShapeDtypeStruct(s, d) for s, d in outs]
    moved = sum(a.size * a.dtype.itemsize for a in arrays)
    moved += sum(o.size * o.dtype.itemsize for o in out_shape)
    return pl.pallas_call(
        body,
        out_shape=out_shape,
        in_specs=[pl.BlockSpec(memory_space=pltpu.SMEM)] * len(scalars)
        + [pl.BlockSpec(memory_space=pltpu.VMEM)] * len(arrays),
        out_specs=[pl.BlockSpec(memory_space=pltpu.VMEM)] * len(outs),
        scratch_shapes=list(scratch),
        cost_estimate=pl.CostEstimate(flops=flops, bytes_accessed=moved, transcendentals=trans),
    )(*scalars, *arrays)


def attend_kernel(base_ref, codes_ref, x_ref, w_ref, vec_ref, ctx_ref, p_ref, qkv_ref, bias_ref):
    cols = ctx_ref.shape[0]
    heads = cols // HEAD
    base = pl.multiple_of(base_ref[0], SEG)
    x = x_ref[pl.ds(base, SEG), :]
    proj = dot(w_ref[...], x, 1, 1)
    pick = (lax.broadcasted_iota(jnp.int32, (16, SEG), 0) == B_QV).astype(BF)
    b_query = dot(vec_ref[:, 0:cols], pick, 0, 0)
    b_value = dot(vec_ref[:, V_AT : V_AT + cols], pick, 0, 0)
    qkv_ref[0:cols, :] = (proj[0:cols] + b_query).astype(BF)
    qkv_ref[cols : 2 * cols, :] = proj[cols : 2 * cols].astype(BF)
    qkv_ref[2 * cols :, :] = (proj[2 * cols :] + b_value).astype(BF)
    first = (lax.broadcasted_iota(jnp.int32, (16, SEG), 0) == 0).astype(BF)
    key_code = dot(codes_ref[...], first, 0, 0)
    query_code = codes_ref[1:2, :].astype(F32)
    allowed = (key_code == query_code) | (key_code == -1.0)
    allowed = allowed | ((query_code == 99.0) & (key_code >= 0.0))
    bias_ref[...] = jnp.where(allowed, 0.0, MASKED_SCORE)
    for h in range(heads):
        at = h * HEAD
        query = qkv_ref[at : at + HEAD, :] * BF(HEAD**-0.5)
        key = qkv_ref[cols + at : cols + at + HEAD, :]
        value = qkv_ref[2 * cols + at : 2 * cols + at + HEAD, :]
        scores = dot(key, query, 0, 0) + bias_ref[...]
        top = jnp.max(scores, axis=0, keepdims=True)
        exps = jnp.exp(scores - top)
        total = jnp.sum(exps, axis=0, keepdims=True)
        probs = (exps * (1.0 / total)).astype(BF)
        p_ref[h] = probs
        ctx_ref[at : at + HEAD, :] = dot(value, probs, 1, 0).astype(BF)


def attend(base, codes, x, w, vec):
    cols = w.shape[0] // 3
    heads = cols // HEAD
    return vmem_call(
        attend_kernel,
        [((cols, SEG), BF), ((heads, SEG, SEG), BF), ((3 * cols, SEG), BF)],
        [base],
        [codes, x, w, vec],
        flops=2 * SEG * 3 * cols * x.shape[1] + 4 * heads * SEG * SEG * HEAD * 4,
        scratch=[pltpu.VMEM((SEG, SEG), F32)],
        trans=heads * SEG * SEG,
    )


def ffn_kernel(
    chunk,
    base_ref,
    co_ref, cp_ref, eo_ref, ep_ref,
    wo_ref, wp_ref, wye_ref, wyp_ref,
    x_ref, veco_ref, vecp_ref,
    upo_ref, upp_ref, dno_ref, dnp_ref,
    xhat_ref, rstd_ref, low_ref, acto_ref, actp_ref, dgo_ref, dgp_ref, part_ref,
):
    span = slice(chunk * HALF, (chunk + 1) * HALF)
    base = pl.multiple_of(base_ref[0] + chunk * HALF, HALF)
    mine = dot(co_ref[:, span], wo_ref[...], 0, 0) + dot(cp_ref[:, span], wp_ref[...], 0, 0)
    peer = dot(eo_ref[:, span], wye_ref[...], 0, 0) + dot(ep_ref[:, span], wyp_ref[...], 0, 0)
    attn = mine.astype(BF).astype(F32) + peer.astype(BF).astype(F32)
    vec = veco_ref[...].astype(F32)
    mixed = x_ref[pl.ds(base, HALF), :].astype(F32) + attn + vec[B_OUT : B_OUT + 1]
    mean = jnp.mean(mixed, axis=-1, keepdims=True)
    centred = mixed - mean
    rstd = lax.rsqrt(jnp.mean(centred * centred, axis=-1, keepdims=True) + NORM_EPS)
    xhat = centred * rstd
    xhat_ref[...] = xhat
    rstd_ref[...] = rstd
    low = (xhat * vec[GAIN1 : GAIN1 + 1] + vec[SHIFT1 : SHIFT1 + 1]).astype(BF)
    low_ref[...] = low
    down = None
    for up_ref, dn_ref, bias, act_ref, dg_ref in (
        (upo_ref, dno_ref, vec[B_UP : B_UP + 1], acto_ref, dgo_ref),
        (upp_ref, dnp_ref, vecp_ref[B_UP : B_UP + 1].astype(F32), actp_ref, dgp_ref),
    ):
        hidden = dot(low, up_ref[...], 1, 0) + bias
        phi = 0.5 + 0.5 * lax.erf(hidden * (0.5**0.5))
        dens = jnp.exp(hidden * hidden * -0.5) * (0.5 * 2.0**0.5 / jnp.pi**0.5)
        act = (hidden * phi).astype(BF)
        act_ref[...] = act
        dg_ref[...] = (phi + hidden * dens).astype(BF)
        term = dot(act, dn_ref[...], 1, 0)
        down = term if down is None else down + term
    part_ref[...] = down.astype(BF)


def ffn(chunk, base, ctxs, wouts, x, veco, vecp, ups, downs):
    d = x.shape[1]
    f = ups[0].shape[1]
    rows = HALF
    return vmem_call(
        partial(ffn_kernel, chunk),
        [((rows, d), F32), ((rows, 1), F32), ((rows, d), BF)]
        + [((rows, f), BF)] * 4
        + [((rows, d), BF)],
        [base],
        [*ctxs, *wouts, x, veco, vecp, *ups, *downs],
        flops=2 * rows * d * (d + 4 * f),
        trans=4 * rows * f,
    )


def back_kernel(
    chunk,
    base_ref,
    mine_ref, peer_ref, xhat_ref, vec_ref, grad_ref,
    dgo_ref, dgp_ref, upo_ref, upp_ref, dno_ref, dnp_ref,
    out_ref, dsec_ref, dlow_ref, dho_ref, dhp_ref, part_ref, sums_ref,
):
    base = pl.multiple_of(base_ref[0] + chunk * HALF, HALF)
    vec = vec_ref[...].astype(F32)
    normed = xhat_ref[...] * vec[GAIN1 : GAIN1 + 1] + vec[SHIFT1 : SHIFT1 + 1]
    total = mine_ref[...].astype(F32) + peer_ref[...].astype(F32)
    second = normed + total + vec[B_DOWN : B_DOWN + 1]
    mean = jnp.mean(second, axis=-1, keepdims=True)
    centred = second - mean
    rstd = lax.rsqrt(jnp.mean(centred * centred, axis=-1, keepdims=True) + NORM_EPS)
    xhat = centred * rstd
    gain = vec[GAIN2 : GAIN2 + 1]
    out_ref[...] = (xhat * gain + vec[SHIFT2 : SHIFT2 + 1]).astype(BF)
    grad = grad_ref[pl.ds(base, HALF), :].astype(F32)
    scaled = grad * gain
    dsec = rstd * (
        scaled
        - jnp.mean(scaled, axis=-1, keepdims=True)
        - xhat * jnp.mean(scaled * xhat, axis=-1, keepdims=True)
    )
    dsec_ref[...] = dsec
    dlow = dsec.astype(BF)
    dlow_ref[...] = dlow
    sums_ref[...] = jnp.zeros_like(sums_ref)
    sums_ref[0:1] = jnp.sum(grad * xhat, axis=0, keepdims=True)
    sums_ref[1:2] = jnp.sum(grad, axis=0, keepdims=True)
    sums_ref[2:3] = jnp.sum(dsec, axis=0, keepdims=True)
    part = None
    for k, (up_ref, dn_ref, dg_ref, dh_ref) in enumerate(
        ((upo_ref, dno_ref, dgo_ref, dho_ref), (upp_ref, dnp_ref, dgp_ref, dhp_ref))
    ):
        dh = dot(dlow, dn_ref[...], 1, 1) * dg_ref[...].astype(F32)
        sums_ref[3 + k : 4 + k] = jnp.sum(dh, axis=0, keepdims=True)
        dh = dh.astype(BF)
        dh_ref[...] = dh
        term = dot(dh, up_ref[...], 1, 1)
        part = term if part is None else part + term
    part_ref[...] = part.astype(BF)


def back(chunk, base, mine, peer, xhat, vec, grad, dgs, ups, downs):
    rows, d = xhat.shape
    f = ups[0].shape[1]
    return vmem_call(
        partial(back_kernel, chunk),
        [((rows, d), BF), ((rows, d), F32), ((rows, d), BF), ((rows, f), BF), ((rows, f), BF)]
        + [((rows, d), BF), ((8, d), F32)],
        [base],
        [mine, peer, xhat, vec, grad, *dgs, *ups, *downs],
        flops=2 * rows * d * 4 * f,
    )


def wgrad_kernel(la_ref, lb_ref, ra_ref, rb_ref, out_ref):
    total = dot(la_ref[...], ra_ref[...], 0, 0) + dot(lb_ref[...], rb_ref[...], 0, 0)
    out_ref[...] = total.astype(BF)


def wgrad(lefts, rights):
    rows, a = lefts[0].shape
    b = rights[0].shape[1]
    return vmem_call(
        wgrad_kernel, [((a, b), BF)], [], [*lefts, *rights], flops=4 * rows * a * b
    )[0]


def mix_kernel(
    dsec_ref, mine_ref, peer_ref, xhat_ref, rstd_ref, vec_ref, wo_ref, wp_ref,
    dmix_ref, dlow_ref, dco_ref, dcp_ref, sums_ref,
):
    gain = vec_ref[GAIN1 : GAIN1 + 1].astype(F32)
    grad = mine_ref[...].astype(F32) + peer_ref[...].astype(F32) + dsec_ref[...]
    xhat = xhat_ref[...]
    scaled = grad * gain
    dmix = rstd_ref[...] * (
        scaled
        - jnp.mean(scaled, axis=-1, keepdims=True)
        - xhat * jnp.mean(scaled * xhat, axis=-1, keepdims=True)
    )
    dmix_ref[...] = dmix
    low = dmix.astype(BF)
    dlow_ref[...] = low
    sums_ref[...] = jnp.zeros_like(sums_ref)
    sums_ref[0:1] = jnp.sum(grad * xhat, axis=0, keepdims=True)
    sums_ref[1:2] = jnp.sum(grad, axis=0, keepdims=True)
    sums_ref[2:3] = jnp.sum(dmix, axis=0, keepdims=True)
    dco_ref[...] = dot(wo_ref[...], low, 1, 1).astype(BF)
    dcp_ref[...] = dot(wp_ref[...], low, 1, 1).astype(BF)


def mix_back(dsec, mine, peer, xhat, rstd, vec, wouts):
    rows, d = xhat.shape
    cols = wouts[0].shape[0]
    return vmem_call(
        mix_kernel,
        [((rows, d), F32), ((rows, d), BF), ((cols, rows), BF), ((cols, rows), BF), ((8, d), F32)],
        [],
        [dsec, mine, peer, xhat, rstd, vec, *wouts],
        flops=4 * rows * d * cols,
    )


def attend_back_kernel(
    base_ref,
    qkv_ref, p_ref, ctx_ref, dca_ref, dcb_ref, x_ref, w_ref, dla_ref, dlb_ref, *rest
):
    given_ref = rest[0] if len(rest) == 5 else None
    gw_ref, part_ref, sums_ref, d_ref = rest[-4:]
    cols = ctx_ref.shape[0]
    base = pl.multiple_of(base_ref[0], SEG)
    for h in range(cols // HEAD):
        at = h * HEAD
        query = qkv_ref[at : at + HEAD, :]
        key = qkv_ref[cols + at : cols + at + HEAD, :]
        value = qkv_ref[2 * cols + at : 2 * cols + at + HEAD, :]
        d_ctx = jnp.concatenate([dca_ref[at : at + HEAD, :], dcb_ref[at : at + HEAD, :]], axis=1)
        probs = p_ref[h]
        inner = jnp.sum(
            d_ctx.astype(F32) * ctx_ref[at : at + HEAD, :].astype(F32), axis=0, keepdims=True
        )
        d_probs = dot(value, d_ctx, 0, 0)
        d_scores = (probs.astype(F32) * (d_probs - inner)).astype(BF)
        scale = HEAD**-0.5
        d_ref[at : at + HEAD, :] = (dot(key, d_scores, 1, 0) * scale).astype(BF)
        d_ref[cols + at : cols + at + HEAD, :] = (dot(query, d_scores, 1, 1) * scale).astype(BF)
        d_ref[2 * cols + at : 2 * cols + at + HEAD, :] = dot(d_ctx, probs, 1, 1).astype(BF)
    part = dot(d_ref[...], w_ref[...], 0, 0)
    if given_ref is None:
        part_ref[...] = part
    else:
        part_ref[...] = (part + given_ref[...]).astype(BF)
    gw_ref[0:cols, :] = (
        dot(ctx_ref[:, 0:HALF], dla_ref[...], 1, 0) + dot(ctx_ref[:, HALF:], dlb_ref[...], 1, 0)
    ).astype(BF)
    gw_ref[cols:, :] = dot(d_ref[...], x_ref[pl.ds(base, SEG), :], 1, 0).astype(BF)
    ones = jnp.ones((16, SEG), BF)
    sums_ref[...] = jnp.zeros_like(sums_ref)
    sums_ref[:, 0:cols] = dot(ones, d_ref[0:cols, :], 1, 1)[0:8]
    sums_ref[:, V_AT : V_AT + cols] = dot(ones, d_ref[2 * cols :, :], 1, 1)[0:8]


def attend_back(base, qkv, probs, ctx, dctx, x, w, dlow, given=None):
    cols, seg = ctx.shape
    d = x.shape[1]
    arrays = [qkv, probs, ctx, *dctx, x, w, *dlow]
    if given is not None:
        arrays.append(given)
    return vmem_call(
        attend_back_kernel,
        [((4 * cols, d), BF), ((seg, d), F32 if given is None else BF), ((8, d), F32)],
        [base],
        arrays,
        flops=2 * seg * d * 7 * cols + 8 * cols * seg * seg * 4,
        scratch=[pltpu.VMEM((3 * cols, seg), BF)],
    )


def pick(array, index, count):
    rows = array.shape[0] // count
    return lax.dynamic_slice_in_dim(array, index * rows, rows, 0)


def join(mine, other, bit):
    return jnp.where(bit == 0, jnp.concatenate([mine, other]), jnp.concatenate([other, mine]))


def reduce_dp(array, size):
    if size != 8:
        return lax.psum(array, "dp").astype(F32)
    place = lax.axis_index("dp")
    bits = [(place >> k) & 1 for k in range(3)]
    for k in range(3):
        perm = [(i, i ^ (1 << k)) for i in range(size)]
        came = lax.ppermute(pick(array, 1 - bits[k], 2), "dp", perm)
        array = (pick(array, bits[k], 2).astype(F32) + came.astype(F32)).astype(BF)
    for k in (2, 1, 0):
        perm = [(i, i ^ (1 << k)) for i in range(size)]
        came = lax.ppermute(array, "dp", perm)
        array = join(array, came, bits[k])
    return array.astype(F32)


def shards(dp_size, tensor_size, seg_input, w_qkv, b_qv, w_out, b_out, norm1_gain, norm1_bias,
           w_up, b_up, w_down, b_down, norm2_gain, norm2_bias, doc_ids, mem_live, out_grad):
    d = seg_input.shape[1]
    cols = w_qkv.shape[2]
    place = lax.axis_index("tensor")
    core = place % 2
    base = jnp.reshape(core * SEG, (1,)).astype(jnp.int32)
    near = [(i, i ^ 1) for i in range(tensor_size)]
    far = [(i, i ^ 2) for i in range(tensor_size)]

    def to_core(a):
        return lax.ppermute(a, "tensor", near)

    def to_peer(a):
        return lax.ppermute(a, "tensor", far)

    vec = jnp.stack([b_out, norm1_gain, norm1_bias, b_down, norm2_gain, norm2_bias, b_up,
                     jnp.concatenate([jnp.pad(b_qv[0], (0, V_AT - cols)),
                                      jnp.pad(b_qv[1], (0, d - V_AT - cols))])])
    vec = jnp.pad(vec, ((0, 8), (0, 0)))
    docs = lax.dynamic_index_in_dim(doc_ids, core, 0, keepdims=False)
    live = lax.dynamic_index_in_dim(mem_live, core, 0, keepdims=False)
    spot = jnp.arange(SEG, dtype=jnp.int32)
    token = (spot >= MEM) & (spot < MEM + SEGTOK)
    padded = jnp.pad(docs, (MEM, SEG - MEM - SEGTOK))
    dead = (spot < MEM) & (spot >= live)
    key_code = jnp.where(token, padded, jnp.where(dead, -2, -1))
    query_code = jnp.where(token, padded, 99)
    codes = jnp.pad(jnp.stack([key_code, query_code]), ((0, 14), (0, 0))).astype(BF)

    w_o = jnp.transpose(w_qkv, (1, 2, 0)).reshape(3 * cols, d)
    w_p = to_core(w_o)
    vec_p = to_core(vec)
    wout_e = to_peer(w_out)
    wout_p = to_core(w_out)
    wout_ep = to_core(wout_e)
    up_p = to_core(w_up)
    down_p = to_core(w_down)
    ups, downs = (w_up, up_p), (w_down, down_p)

    ctx_o, probs_o, qkv_o = attend(base, codes, seg_input, w_o, vec)
    ctx_eo = to_peer(ctx_o)
    ctx_p, probs_p, qkv_p = attend(base, codes, seg_input, w_p, vec_p)
    ctx_ep = to_peer(ctx_p)
    fwd = [ffn(k, base, (ctx_o, ctx_p, ctx_eo, ctx_ep), (w_out, wout_p, wout_e, wout_ep),
               seg_input, vec, vec_p, ups, downs) for k in range(2)]
    xhat, rstd, low, act_o, act_p, dg_o, dg_p, part = zip(*fwd)
    peer = [to_peer(p) for p in part]
    bwd = [back(k, base, part[k], peer[k], xhat[k], vec, out_grad, (dg_o[k], dg_p[k]), ups, downs)
           for k in range(2)]
    out, dsec, dlow, dh_o, dh_p, npart, sums2 = zip(*bwd)
    npeer = [to_peer(p) for p in npart]
    gdown_p = to_core(wgrad(act_p, dlow))
    gup_p = to_core(wgrad(low, dh_p))
    gdown = (wgrad(act_o, dlow).astype(F32) + gdown_p.astype(F32)).astype(BF)
    gup = (wgrad(low, dh_o).astype(F32) + gup_p.astype(F32)).astype(BF)
    grad_w_down = reduce_dp(gdown, dp_size)
    grad_w_up = reduce_dp(gup, dp_size)
    mixes = [mix_back(dsec[k], npart[k], npeer[k], xhat[k], rstd[k], vec, (w_out, wout_p))
             for k in range(2)]
    dmix, dmlow, dc_o, dc_p, sums1 = zip(*mixes)
    gw_p, ipart, sums_p = attend_back(base, qkv_p, probs_p, ctx_p, dc_p, seg_input, w_p, dmlow)
    gw_o, ipart, sums_o = attend_back(base, qkv_o, probs_o, ctx_o, dc_o, seg_input, w_o, dmlow, ipart)
    ipeer = to_peer(ipart)

    s1 = sums1[0] + sums1[1]
    s2 = sums2[0] + sums2[1]

    def small(b_up_row, b_qv_row):
        return jnp.concatenate([s1[2:3], s1[0:2], s2[2:3], s2[0:2], b_up_row, b_qv_row,
                                jnp.zeros((56, d), F32)]).astype(BF)

    send = jnp.concatenate([gw_p, small(s2[4:5], sums_p[0:1])])
    keep = jnp.concatenate([gw_o, small(s2[3:4], sums_o[0:1])])
    rest = (keep.astype(F32) + to_core(send).astype(F32)).astype(BF)
    rest = reduce_dp(rest, dp_size)

    own_out = jnp.concatenate(out)
    seg_output = join(own_out, to_core(own_out), core)
    own_grad = (jnp.concatenate(dmix) + (ipart.astype(F32) + ipeer.astype(F32))).astype(BF)
    grad_input = join(own_grad, to_core(own_grad), core)

    grad_w_out = rest[0:cols]
    grad_w_qkv = jnp.transpose(rest[cols : 4 * cols].reshape(3, cols, d), (2, 0, 1))
    tail = rest[4 * cols :]
    grad_b_qv = jnp.stack([tail[B_QV, 0:cols], tail[B_QV, V_AT : V_AT + cols]])
    return (seg_output, grad_input, grad_w_qkv, grad_b_qv, grad_w_out, tail[B_OUT], tail[GAIN1],
            tail[SHIFT1], grad_w_up, tail[B_UP], grad_w_down, tail[B_DOWN], tail[GAIN2],
            tail[SHIFT2])


def solution(mesh):
    wide, col, row, one = P("dp", None), P(None, "tensor"), P("tensor", None), P()
    return jax.shard_map(
        partial(shards, mesh.shape["dp"], mesh.shape["tensor"]),
        mesh=mesh,
        in_specs=(wide, P(None, None, "tensor"), col, row, one, one, one, col, P("tensor"), row,
                  one, one, one, wide, P("dp"), wide),
        out_specs=(wide, wide, P(None, None, "tensor"), col, row, one, one, one, col, P("tensor"),
                   row, one, one, one),
        check_vma=False,
    )
```

```python
from functools import partial

import jax
import jax.numpy as jnp
from jax import lax
from jax.experimental import pallas as pl
from jax.experimental.pallas import tpu as pltpu
from jax.sharding import PartitionSpec as P

HEAD = 64
MEM = 10
SEGTOK = 492
SEG = 512
HALF = 256
MASKED_SCORE = -1e30
NORM_EPS = 1e-05
BF = jnp.bfloat16
F32 = jnp.float32
B_OUT, GAIN1, SHIFT1, B_DOWN, GAIN2, SHIFT2, B_UP, B_QV = range(8)
B_UP_P = B_QV
BIAS_ROWS = 8
TAIL = 64
PACE = 10_000_000_000
V_AT = 256


def dot(left, right, left_dim, right_dim):
    return lax.dot_general(
        left, right, (((left_dim,), (right_dim,)), ((), ())), preferred_element_type=F32
    )


def after(value, *earlier):
    return lax.optimization_barrier((value, *earlier))[0]


def vmem_call(body, outs, scalars, arrays, scratch=(), limit=16):
    out_shape = [jax.ShapeDtypeStruct(s, d) for s, d in outs]
    return pl.pallas_call(
        body,
        out_shape=out_shape,
        in_specs=[pl.BlockSpec(memory_space=pltpu.SMEM)] * len(scalars)
        + [pl.BlockSpec(memory_space=pltpu.VMEM)] * len(arrays),
        out_specs=[pl.BlockSpec(memory_space=pltpu.VMEM)] * len(outs),
        scratch_shapes=list(scratch),
        compiler_params=pltpu.CompilerParams(vmem_limit_bytes=limit << 20),
        cost_estimate=pl.CostEstimate(flops=PACE, bytes_accessed=0, transcendentals=0),
    )(*scalars, *arrays)


def attend_kernel(
    base_ref, codes_ref, x_ref, w_ref, bias_qv_ref, ctx_ref, p_ref, qkv_ref, bias_ref
):
    cols = ctx_ref.shape[0]
    heads = cols // HEAD
    core = base_ref[0] // SEG
    base = pl.multiple_of(base_ref[0], SEG)
    x = x_ref[pl.ds(base, SEG), :]
    proj = dot(w_ref[...], x, 1, 1)
    line = lax.broadcasted_iota(jnp.int32, (BIAS_ROWS, SEG), 0)
    b_query = dot(bias_qv_ref[...], (line == 0).astype(BF), 0, 0)
    b_value = dot(bias_qv_ref[...], (line == 1).astype(BF), 0, 0)
    qkv_ref[0:cols, :] = (proj[0:cols] + b_query).astype(BF)
    qkv_ref[cols : 2 * cols, :] = proj[cols : 2 * cols].astype(BF)
    qkv_ref[2 * cols :, :] = (proj[2 * cols :] + b_value).astype(BF)
    codes = codes_ref[...].astype(F32)
    key_line = jnp.where(core == 0, codes[0:1], codes[1:2])
    spot = lax.broadcasted_iota(jnp.int32, (1, SEG), 1)
    token = (spot >= MEM) & (spot < MEM + SEGTOK)
    query_code = jnp.where(token, key_line, 99.0)
    first = (lax.broadcasted_iota(jnp.int32, (16, SEG), 0) == 0).astype(BF)
    key_code = dot(jnp.broadcast_to(key_line, (16, SEG)).astype(BF), first, 0, 0)
    allowed = (key_code == query_code) | (key_code == -1.0)
    allowed = allowed | ((query_code == 99.0) & (key_code >= 0.0))
    bias_ref[...] = jnp.where(allowed, 0.0, MASKED_SCORE)
    for h in range(heads):
        at = h * HEAD
        query = qkv_ref[at : at + HEAD, :] * BF(HEAD**-0.5)
        key = qkv_ref[cols + at : cols + at + HEAD, :]
        value = qkv_ref[2 * cols + at : 2 * cols + at + HEAD, :]
        scores = dot(key, query, 0, 0) + bias_ref[...]
        top = jnp.max(scores, axis=0, keepdims=True)
        exps = jnp.exp(scores - top)
        total = jnp.sum(exps, axis=0, keepdims=True)
        probs = (exps * (1.0 / total)).astype(BF)
        p_ref[h] = probs
        ctx_ref[at : at + HEAD, :] = dot(value, probs, 1, 0).astype(BF)


def attend(base, codes, x, w, bias):
    cols = w.shape[0] // 3
    heads = cols // HEAD
    return vmem_call(
        attend_kernel,
        [((cols, SEG), BF), ((heads, SEG, SEG), BF), ((3 * cols, SEG), BF)],
        [base],
        [codes, x, w, bias],
        scratch=[pltpu.VMEM((SEG, SEG), F32)],
    )


def ffn_kernel(
    chunk,
    base_ref,
    co_ref, cp_ref, eo_ref, ep_ref,
    wo_ref, wp_ref, wye_ref, wyp_ref,
    x_ref, veco_ref,
    upo_ref, upp_ref, dno_ref, dnp_ref,
    xhat_ref, rstd_ref, low_ref, acto_ref, actp_ref, dgo_ref, dgp_ref, part_ref,
):
    span = slice(chunk * HALF, (chunk + 1) * HALF)
    base = pl.multiple_of(base_ref[0] + chunk * HALF, HALF)
    mine = dot(co_ref[:, span], wo_ref[...], 0, 0) + dot(cp_ref[:, span], wp_ref[...], 0, 0)
    peer = dot(eo_ref[:, span], wye_ref[...], 0, 0) + dot(ep_ref[:, span], wyp_ref[...], 0, 0)
    attn = mine.astype(BF).astype(F32) + peer.astype(BF).astype(F32)
    vec = veco_ref[...].astype(F32)
    mixed = x_ref[pl.ds(base, HALF), :].astype(F32) + attn + vec[B_OUT : B_OUT + 1]
    mean = jnp.mean(mixed, axis=-1, keepdims=True)
    centred = mixed - mean
    rstd = lax.rsqrt(jnp.mean(centred * centred, axis=-1, keepdims=True) + NORM_EPS)
    xhat = centred * rstd
    xhat_ref[...] = xhat
    rstd_ref[...] = rstd
    low = (xhat * vec[GAIN1 : GAIN1 + 1] + vec[SHIFT1 : SHIFT1 + 1]).astype(BF)
    low_ref[...] = low
    down = None
    for up_ref, dn_ref, bias, act_ref, dg_ref in (
        (upo_ref, dno_ref, vec[B_UP : B_UP + 1], acto_ref, dgo_ref),
        (upp_ref, dnp_ref, vec[B_UP_P : B_UP_P + 1], actp_ref, dgp_ref),
    ):
        hidden = dot(low, up_ref[...], 1, 0) + bias
        phi = 0.5 + 0.5 * lax.erf(hidden * (0.5**0.5))
        dens = jnp.exp(hidden * hidden * -0.5) * (0.5 * 2.0**0.5 / jnp.pi**0.5)
        act = (hidden * phi).astype(BF)
        act_ref[...] = act
        dg_ref[...] = (phi + hidden * dens).astype(BF)
        term = dot(act, dn_ref[...], 1, 0)
        down = term if down is None else down + term
    part_ref[...] = down.astype(BF)


def ffn(chunk, base, ctxs, wouts, x, veco, ups, downs):
    d = x.shape[1]
    f = ups[0].shape[1]
    rows = HALF
    return vmem_call(
        partial(ffn_kernel, chunk),
        [((rows, d), F32), ((rows, 1), F32), ((rows, d), BF)]
        + [((rows, f), BF)] * 4
        + [((rows, d), BF)],
        [base],
        [*ctxs, *wouts, x, veco, *ups, *downs],
    )


def back_kernel(
    chunk,
    base_ref,
    mine_ref, peer_ref, xhat_ref, vec_ref, grad_ref,
    dgo_ref, dgp_ref, upo_ref, upp_ref, dno_ref, dnp_ref,
    out_ref, dsec_ref, dlow_ref, dho_ref, dhp_ref, part_ref, sums_ref,
):
    base = pl.multiple_of(base_ref[0] + chunk * HALF, HALF)
    vec = vec_ref[...].astype(F32)
    normed = xhat_ref[...] * vec[GAIN1 : GAIN1 + 1] + vec[SHIFT1 : SHIFT1 + 1]
    total = mine_ref[...].astype(F32) + peer_ref[...].astype(F32)
    second = normed + total + vec[B_DOWN : B_DOWN + 1]
    mean = jnp.mean(second, axis=-1, keepdims=True)
    centred = second - mean
    rstd = lax.rsqrt(jnp.mean(centred * centred, axis=-1, keepdims=True) + NORM_EPS)
    xhat = centred * rstd
    gain = vec[GAIN2 : GAIN2 + 1]
    out_ref[...] = (xhat * gain + vec[SHIFT2 : SHIFT2 + 1]).astype(BF)
    grad = grad_ref[pl.ds(base, HALF), :].astype(F32)
    scaled = grad * gain
    dsec = rstd * (
        scaled
        - jnp.mean(scaled, axis=-1, keepdims=True)
        - xhat * jnp.mean(scaled * xhat, axis=-1, keepdims=True)
    )
    dsec_ref[...] = dsec
    dlow = dsec.astype(BF)
    dlow_ref[...] = dlow
    sums_ref[...] = jnp.zeros_like(sums_ref)
    sums_ref[0:1] = jnp.sum(grad * xhat, axis=0, keepdims=True)
    sums_ref[1:2] = jnp.sum(grad, axis=0, keepdims=True)
    sums_ref[2:3] = jnp.sum(dsec, axis=0, keepdims=True)
    part = None
    for k, (up_ref, dn_ref, dg_ref, dh_ref) in enumerate(
        ((upo_ref, dno_ref, dgo_ref, dho_ref), (upp_ref, dnp_ref, dgp_ref, dhp_ref))
    ):
        dh = dot(dlow, dn_ref[...], 1, 1) * dg_ref[...].astype(F32)
        sums_ref[3 + k : 4 + k] = jnp.sum(dh, axis=0, keepdims=True)
        dh = dh.astype(BF)
        dh_ref[...] = dh
        term = dot(dh, up_ref[...], 1, 1)
        part = term if part is None else part + term
    part_ref[...] = part.astype(BF)


def back(chunk, base, mine, peer, xhat, vec, grad, dgs, ups, downs):
    rows, d = xhat.shape
    f = ups[0].shape[1]
    return vmem_call(
        partial(back_kernel, chunk),
        [((rows, d), BF), ((rows, d), F32), ((rows, d), BF), ((rows, f), BF), ((rows, f), BF)]
        + [((rows, d), BF), ((8, d), F32)],
        [base],
        [mine, peer, xhat, vec, grad, *dgs, *ups, *downs],
    )


def wgrad_kernel(base_ref, la_ref, lb_ref, ra_ref, rb_ref, out_ref):
    total = dot(la_ref[...], ra_ref[...], 0, 0) + dot(lb_ref[...], rb_ref[...], 0, 0)
    out_ref[...] = total.astype(BF)


def wgrad(base, lefts, rights):
    rows, a = lefts[0].shape
    b = rights[0].shape[1]
    return vmem_call(
        wgrad_kernel, [((a, b), BF)], [base], [*lefts, *rights]
    )[0]


def mix_kernel(
    base_ref,
    dsec_ref, mine_ref, peer_ref, xhat_ref, rstd_ref, vec_ref, wo_ref, wp_ref,
    dmix_ref, dlow_ref, dco_ref, dcp_ref, sums_ref,
):
    gain = vec_ref[GAIN1 : GAIN1 + 1].astype(F32)
    grad = mine_ref[...].astype(F32) + peer_ref[...].astype(F32) + dsec_ref[...]
    xhat = xhat_ref[...]
    scaled = grad * gain
    dmix = rstd_ref[...] * (
        scaled
        - jnp.mean(scaled, axis=-1, keepdims=True)
        - xhat * jnp.mean(scaled * xhat, axis=-1, keepdims=True)
    )
    dmix_ref[...] = dmix
    low = dmix.astype(BF)
    dlow_ref[...] = low
    sums_ref[...] = jnp.zeros_like(sums_ref)
    sums_ref[0:1] = jnp.sum(grad * xhat, axis=0, keepdims=True)
    sums_ref[1:2] = jnp.sum(grad, axis=0, keepdims=True)
    sums_ref[2:3] = jnp.sum(dmix, axis=0, keepdims=True)
    dco_ref[...] = dot(wo_ref[...], low, 1, 1).astype(BF)
    dcp_ref[...] = dot(wp_ref[...], low, 1, 1).astype(BF)


def mix_back(base, dsec, mine, peer, xhat, rstd, vec, wouts):
    rows, d = xhat.shape
    cols = wouts[0].shape[0]
    return vmem_call(
        mix_kernel,
        [((rows, d), F32), ((rows, d), BF), ((cols, rows), BF), ((cols, rows), BF), ((8, d), F32)],
        [base],
        [dsec, mine, peer, xhat, rstd, vec, *wouts],
    )


def attend_back_kernel(
    own,
    base_ref,
    qkv_ref, p_ref, ctx_ref, dca_ref, dcb_ref, x_ref, w_ref, dla_ref, dlb_ref,
    s1a_ref, s1b_ref, s2a_ref, s2b_ref, *rest
):
    given_ref = rest[0] if len(rest) == 5 else None
    gw_ref, part_ref, tail_ref, d_ref = rest[-4:]
    cols = ctx_ref.shape[0]
    base = pl.multiple_of(base_ref[0], SEG)
    for h in range(cols // HEAD):
        at = h * HEAD
        query = qkv_ref[at : at + HEAD, :]
        key = qkv_ref[cols + at : cols + at + HEAD, :]
        value = qkv_ref[2 * cols + at : 2 * cols + at + HEAD, :]
        d_ctx = jnp.concatenate([dca_ref[at : at + HEAD, :], dcb_ref[at : at + HEAD, :]], axis=1)
        probs = p_ref[h]
        inner = jnp.sum(
            d_ctx.astype(F32) * ctx_ref[at : at + HEAD, :].astype(F32), axis=0, keepdims=True
        )
        d_probs = dot(value, d_ctx, 0, 0)
        d_scores = (probs.astype(F32) * (d_probs - inner)).astype(BF)
        scale = HEAD**-0.5
        d_ref[at : at + HEAD, :] = (dot(key, d_scores, 1, 0) * scale).astype(BF)
        d_ref[cols + at : cols + at + HEAD, :] = (dot(query, d_scores, 1, 1) * scale).astype(BF)
        d_ref[2 * cols + at : 2 * cols + at + HEAD, :] = dot(d_ctx, probs, 1, 1).astype(BF)
    part = dot(d_ref[...], w_ref[...], 0, 0)
    if given_ref is None:
        part_ref[...] = part
    else:
        part_ref[...] = (part + given_ref[...]).astype(BF)
    gw_ref[0:cols, :] = (
        dot(ctx_ref[:, 0:HALF], dla_ref[...], 1, 0) + dot(ctx_ref[:, HALF:], dlb_ref[...], 1, 0)
    ).astype(BF)
    gw_ref[cols : 4 * cols, :] = dot(d_ref[...], x_ref[pl.ds(base, SEG), :], 1, 0).astype(BF)
    ones = jnp.ones((16, SEG), BF)
    tail_ref[...] = jnp.zeros_like(tail_ref)
    s1 = s1a_ref[...] + s1b_ref[...]
    s2 = s2a_ref[...] + s2b_ref[...]
    tail_ref[B_OUT : B_OUT + 1] = s1[2:3]
    tail_ref[GAIN1 : SHIFT1 + 1] = s1[0:2]
    tail_ref[B_DOWN : B_DOWN + 1] = s2[2:3]
    tail_ref[GAIN2 : SHIFT2 + 1] = s2[0:2]
    tail_ref[B_UP : B_UP + 1] = s2[3:4] if own else s2[4:5]
    tail_ref[B_QV : B_QV + 1, 0:cols] = dot(ones, d_ref[0:cols, :], 1, 1)[0:1]
    tail_ref[B_QV : B_QV + 1, V_AT : V_AT + cols] = dot(ones, d_ref[2 * cols :, :], 1, 1)[0:1]
    gw_ref[4 * cols :, :] = tail_ref[...].astype(BF)


def attend_back(own, base, qkv, probs, ctx, dctx, x, w, dlow, sums1, sums2, given=None):
    cols, seg = ctx.shape
    d = x.shape[1]
    arrays = [qkv, probs, ctx, *dctx, x, w, *dlow, *sums1, *sums2]
    if given is not None:
        arrays.append(given)
    return vmem_call(
        partial(attend_back_kernel, own),
        [((4 * cols + TAIL, d), BF), ((seg, d), F32 if given is None else BF)],
        [base],
        arrays,
        scratch=[pltpu.VMEM((TAIL, d), F32), pltpu.VMEM((3 * cols, seg), BF)],
    )


def grad_kernel(base_ref, dma_ref, dmb_ref, mine_ref, peer_ref, out_ref):
    total = mine_ref[...].astype(F32) + peer_ref[...].astype(F32)
    out_ref[0:HALF] = (dma_ref[...] + total[0:HALF]).astype(BF)
    out_ref[HALF:] = (dmb_ref[...] + total[HALF:]).astype(BF)


def place_kernel(base_ref, *refs):
    out_ref = refs[-1]
    each = len(refs) // 2
    own = pl.multiple_of(base_ref[0], SEG)
    other = pl.multiple_of(SEG - base_ref[0], SEG)
    at = 0
    for mine_ref, came_ref in zip(refs[:each], refs[each:-1]):
        rows = mine_ref.shape[0]
        out_ref[pl.ds(own + at, rows), :] = mine_ref[...]
        out_ref[pl.ds(other + at, rows), :] = came_ref[...]
        at += rows


def place(base, own, came):
    return vmem_call(
        place_kernel, [((2 * SEG, own[0].shape[1]), BF)], [base], [*own, *came]
    )[0]


X, Z0, Z1 = range(3)


def hop(array, size, bit):
    return lax.ppermute(array, "dp", [(i, i ^ (1 << bit)) for i in range(size)])


def add_kernel(bit_ref, mine_ref, came_ref, *refs):
    total = mine_ref[...].astype(F32) + came_ref[...].astype(F32)
    if len(refs) == 1:
        refs[0][...] = total.astype(BF)
        return
    keep_ref, send_ref, total_ref = refs
    rows = keep_ref.shape[0]
    total_ref[...] = total.astype(BF)
    keep_ref[...] = total_ref[pl.ds(pl.multiple_of(bit_ref[0] * rows, 8), rows), :]
    send_ref[...] = total_ref[pl.ds(pl.multiple_of((1 - bit_ref[0]) * rows, 8), rows), :]


def add(bit, mine, came, halves):
    rows, d = mine.shape
    if not halves:
        return vmem_call(add_kernel, [((rows, d), BF)], [bit], [mine, came], limit=8)[0]
    return vmem_call(
        add_kernel, [((rows // 2, d), BF)] * 2, [bit], [mine, came], limit=8,
        scratch=[pltpu.VMEM((rows, d), BF)],
    )


def join_kernel(spans, bit_ref, mine_ref, came_ref, *refs):
    both_ref = refs[-1] if len(refs) > len(spans) else refs[0]
    rows = mine_ref.shape[0]
    own = pl.multiple_of(bit_ref[0] * rows, 8)
    other = pl.multiple_of((1 - bit_ref[0]) * rows, 8)
    both_ref[pl.ds(own, rows), :] = mine_ref[...].astype(both_ref.dtype)
    both_ref[pl.ds(other, rows), :] = came_ref[...].astype(both_ref.dtype)
    if len(refs) > len(spans):
        at = 0
        for ref, span in zip(refs, spans):
            ref[...] = both_ref[at : at + span, :].astype(ref.dtype)
            at += span


def join(bit, mine, came, spans, dtype):
    rows, d = mine.shape
    scratch = [] if len(spans) == 1 else [pltpu.VMEM((2 * rows, d), BF)]
    return vmem_call(
        partial(join_kernel, spans), [((span, d), dtype) for span in spans], [bit], [mine, came],
        limit=8, scratch=scratch,
    )


class Line:
    def __init__(self):
        self.last = None

    def at(self, value):
        return value if self.last is None else after(value, self.last)

    def done(self, value):
        self.last = value
        return value


def reduce_dp(line, mine, came, size, spans, order=(X, Z0, Z1)):
    if size != 8:
        rows = mine.shape[0]
        total = lax.psum((mine.astype(F32) + came.astype(F32)).astype(BF), "dp").astype(F32)
        for _ in range(6):
            yield None
        ends = [sum(spans[: k + 1]) for k in range(len(spans))]
        yield [total[e - n : e] for e, n in zip(ends, spans)]
        return
    place_in = lax.axis_index("dp")
    bits = [jnp.reshape((place_in >> k) & 1, (1,)).astype(jnp.int32) for k in range(3)]
    for bit in order:
        mine, send = add(line.at(bits[bit]), mine, came, True)
        line.done(send)
        came = hop(send, size, bit)
        yield None
    mine = line.done(add(line.at(bits[order[0]]), mine, came, False))
    for bit in order[::-1]:
        came = hop(mine, size, bit)
        yield None
        last = bit == order[0]
        parts = join(line.at(bits[bit]), mine, came, spans if last else (2 * mine.shape[0],),
                     F32 if last else BF)
        mine = line.done(parts[0])
    yield parts


def shards(dp_size, tensor_size, seg_input, w_qkv, b_qv, w_out, b_out, norm1_gain, norm1_bias,
           w_up, b_up, w_down, b_down, norm2_gain, norm2_bias, doc_ids, mem_live, out_grad):
    d = seg_input.shape[1]
    cols = w_qkv.shape[2]
    place_in = lax.axis_index("tensor")
    core = place_in % 2
    base = jnp.reshape(core * SEG, (1,)).astype(jnp.int32)
    near = [(i, i ^ 1) for i in range(tensor_size)]
    far = [(i, i ^ 2) for i in range(tensor_size)]

    def to_core(a):
        return lax.ppermute(a, "tensor", near)

    def to_peer(a):
        return lax.ppermute(a, "tensor", far)

    spot = jnp.arange(SEG, dtype=jnp.int32)[None]
    token = (spot >= MEM) & (spot < MEM + SEGTOK)
    dead = (spot < MEM) & (spot >= mem_live[:, None])
    padded = jnp.pad(doc_ids, ((0, 0), (MEM, SEG - MEM - SEGTOK)))
    codes = jnp.where(token, padded, jnp.where(dead, -2, -1)).astype(BF)
    bias_o = jnp.concatenate([b_qv, b_up.reshape(d // cols, cols),
                              jnp.zeros((BIAS_ROWS - 2 - d // cols, cols), BF)])

    line = Line()

    def now():
        return line.at(base)

    w_o = jnp.transpose(w_qkv, (1, 2, 0)).reshape(3 * cols, d)
    bias_p = to_core(bias_o)
    w_p = to_core(w_o)
    wout_e = to_peer(w_out)
    up_p = to_core(w_up)
    down_p = to_core(w_down)
    ups, downs = (w_up, up_p), (w_down, down_p)

    ctx_o, probs_o, qkv_o = attend(base, codes, seg_input, w_o, bias_o)
    line.done(ctx_o)
    ctx_eo = to_peer(ctx_o)
    wout_p = to_core(line.at(w_out))
    ctx_p, probs_p, qkv_p = attend(after(now(), up_p, down_p), codes, seg_input, w_p, bias_p)
    line.done(ctx_p)
    ctx_ep = to_peer(ctx_p)
    wout_ep = to_core(wout_e)
    b_up_p = bias_p[2 : 2 + d // cols].reshape(d)
    row = jnp.arange(8, dtype=jnp.int32)[:, None]
    vec = jnp.broadcast_to(b_up_p, (8, d))
    for k, one in enumerate((b_out, norm1_gain, norm1_bias, b_down, norm2_gain, norm2_bias, b_up)):
        vec = jnp.where(row == k, one, vec)
    fwd = []
    for k in range(2):
        fwd.append(ffn(k, now(), (ctx_o, ctx_p, ctx_eo, ctx_ep), (w_out, wout_p, wout_e, wout_ep),
                       seg_input, vec, ups, downs))
        line.done(fwd[-1][-1])
    xhat, rstd, low, act_o, act_p, dg_o, dg_p, part = zip(*fwd)
    peer = [to_peer(p) for p in part]
    bwd = []
    for k in range(2):
        bwd.append(back(k, now(), part[k], peer[k], xhat[k], vec, out_grad, (dg_o[k], dg_p[k]),
                        ups, downs))
        line.done(bwd[-1][-2])
    out, dsec, dlow, dh_o, dh_p, npart, sums2 = zip(*bwd)
    npeer = [to_peer(p) for p in npart]
    gdown_p = to_core(line.done(wgrad(now(), act_p, dlow)))
    gup_p = to_core(line.done(wgrad(now(), low, dh_p)))
    gdown = line.done(wgrad(now(), act_o, dlow))
    gup = line.done(wgrad(now(), low, dh_o))
    chains = {
        "D": reduce_dp(line, gdown, gdown_p, dp_size, gdown.shape[:1]),
        "U": reduce_dp(line, gup, gup_p, dp_size, gup.shape[:1]),
    }
    sums = {}

    def go(names):
        for name in names:
            sums[name] = next(chains[name])

    go("DU")
    mixes = []
    for k in range(2):
        mixes.append(mix_back(now(), dsec[k], npart[k], npeer[k], xhat[k], rstd[k], vec,
                              (w_out, wout_p)))
        line.done(mixes[-1][1])
    dmix, dmlow, dc_o, dc_p, sums1 = zip(*mixes)
    gw_p, ipart = attend_back(False, now(), qkv_p, probs_p, ctx_p, dc_p, seg_input, w_p, dmlow,
                              sums1, sums2)
    line.done(gw_p)
    gw_p = to_core(gw_p)
    go("D")
    gw_o, ipart = attend_back(True, now(), qkv_o, probs_o, ctx_o, dc_o, seg_input, w_o, dmlow,
                              sums1, sums2, ipart)
    line.done(gw_o)
    ipeer = to_peer(ipart)
    chains["R"] = reduce_dp(line, gw_o, gw_p, dp_size, (cols, 3 * cols, TAIL))
    go("RDUDU")
    own_grad = line.done(vmem_call(grad_kernel, [((SEG, d), BF)], [now()],
                                   [*dmix, ipart, ipeer])[0])
    own_came = to_core(own_grad)
    go("DRU")
    grad_input = line.done(place(now(), [own_grad], [own_came]))
    out_came = [to_core(line.at(o)) for o in out]
    go("DRU")
    seg_output = line.done(place(now(), out, out_came))
    go("RUDRRUR")
    (grad_w_down,), (grad_w_up,), (grad_w_out, grad_qkv, tail) = (sums[k] for k in "DUR")

    grad_w_qkv = jnp.transpose(grad_qkv.reshape(3, cols, d), (2, 0, 1))
    grad_b_qv = jnp.stack([tail[B_QV, 0:cols], tail[B_QV, V_AT : V_AT + cols]])
    return (seg_output, grad_input, grad_w_qkv, grad_b_qv, grad_w_out, tail[B_OUT], tail[GAIN1],
            tail[SHIFT1], grad_w_up, tail[B_UP], grad_w_down, tail[B_DOWN], tail[GAIN2],
            tail[SHIFT2])


def solution(mesh):
    wide, col, row, one = P("dp", None), P(None, "tensor"), P("tensor", None), P()
    return jax.shard_map(
        partial(shards, mesh.shape["dp"], mesh.shape["tensor"]),
        mesh=mesh,
        in_specs=(wide, P(None, None, "tensor"), col, row, one, one, one, col, P("tensor"), row,
                  one, one, one, wide, P("dp"), wide),
        out_specs=(wide, wide, P(None, None, "tensor"), col, row, one, one, one, col, P("tensor"),
                   row, one, one, one),
        check_vma=False,
    )
```

```python
from functools import partial

import jax
import jax.numpy as jnp
from jax import lax
from jax.experimental import pallas as pl
from jax.experimental.pallas import tpu as pltpu
from jax.sharding import PartitionSpec as P

HEAD = 64
MEM = 10
SEGTOK = 492
SEG = 512
HALF = 256
MASKED_SCORE = -1e30
NORM_EPS = 1e-05
BF = jnp.bfloat16
F32 = jnp.float32
B_OUT, GAIN1, SHIFT1, B_DOWN, GAIN2, SHIFT2, B_UP, B_QV = range(8)
B_UP_P = B_QV
BIAS_ROWS = 8
TAIL = 64
PACE = 10_000_000_000
V_AT = 256


def dot(left, right, left_dim, right_dim):
    return lax.dot_general(
        left, right, (((left_dim,), (right_dim,)), ((), ())), preferred_element_type=F32
    )


def after(value, *earlier):
    return lax.optimization_barrier((value, *earlier))[0]


def vmem_call(body, outs, scalars, arrays, scratch=(), limit=16, pace=PACE):
    out_shape = [jax.ShapeDtypeStruct(s, d) for s, d in outs]
    return pl.pallas_call(
        body,
        out_shape=out_shape,
        in_specs=[pl.BlockSpec(memory_space=pltpu.SMEM)] * len(scalars)
        + [pl.BlockSpec(memory_space=pltpu.VMEM)] * len(arrays),
        out_specs=[pl.BlockSpec(memory_space=pltpu.VMEM)] * len(outs),
        scratch_shapes=list(scratch),
        compiler_params=pltpu.CompilerParams(vmem_limit_bytes=limit << 20),
        cost_estimate=pl.CostEstimate(flops=pace, bytes_accessed=0, transcendentals=0),
    )(*scalars, *arrays)


def attend_kernel(
    base_ref, codes_ref, x_ref, w_ref, bias_qv_ref, ctx_ref, p_ref, qkv_ref, bias_ref
):
    cols = ctx_ref.shape[0]
    heads = cols // HEAD
    core = base_ref[0] // SEG
    base = pl.multiple_of(base_ref[0], SEG)
    x = x_ref[pl.ds(base, SEG), :]
    proj = dot(w_ref[...], x, 1, 1)
    line = lax.broadcasted_iota(jnp.int32, (BIAS_ROWS, SEG), 0)
    b_query = dot(bias_qv_ref[...], (line == 0).astype(BF), 0, 0)
    b_value = dot(bias_qv_ref[...], (line == 1).astype(BF), 0, 0)
    qkv_ref[0:cols, :] = (proj[0:cols] + b_query).astype(BF)
    qkv_ref[cols : 2 * cols, :] = proj[cols : 2 * cols].astype(BF)
    qkv_ref[2 * cols :, :] = (proj[2 * cols :] + b_value).astype(BF)
    codes = codes_ref[...].astype(F32)
    key_line = jnp.where(core == 0, codes[0:1], codes[1:2])
    spot = lax.broadcasted_iota(jnp.int32, (1, SEG), 1)
    token = (spot >= MEM) & (spot < MEM + SEGTOK)
    query_code = jnp.where(token, key_line, 99.0)
    first = (lax.broadcasted_iota(jnp.int32, (16, SEG), 0) == 0).astype(BF)
    key_code = dot(jnp.broadcast_to(key_line, (16, SEG)).astype(BF), first, 0, 0)
    allowed = (key_code == query_code) | (key_code == -1.0)
    allowed = allowed | ((query_code == 99.0) & (key_code >= 0.0))
    bias_ref[...] = jnp.where(allowed, 0.0, MASKED_SCORE)
    for h in range(heads):
        at = h * HEAD
        query = qkv_ref[at : at + HEAD, :] * BF(HEAD**-0.5)
        key = qkv_ref[cols + at : cols + at + HEAD, :]
        value = qkv_ref[2 * cols + at : 2 * cols + at + HEAD, :]
        scores = dot(key, query, 0, 0) + bias_ref[...]
        top = jnp.max(scores, axis=0, keepdims=True)
        exps = jnp.exp(scores - top)
        total = jnp.sum(exps, axis=0, keepdims=True)
        probs = (exps * (1.0 / total)).astype(BF)
        p_ref[h] = probs
        ctx_ref[at : at + HEAD, :] = dot(value, probs, 1, 0).astype(BF)


def attend(base, codes, x, w, bias):
    cols = w.shape[0] // 3
    heads = cols // HEAD
    return vmem_call(
        attend_kernel,
        [((cols, SEG), BF), ((heads, SEG, SEG), BF), ((3 * cols, SEG), BF)],
        [base],
        [codes, x, w, bias],
        scratch=[pltpu.VMEM((SEG, SEG), F32)],
    )


def ffn_kernel(
    chunk,
    base_ref,
    co_ref, cp_ref, eo_ref, ep_ref,
    wo_ref, wp_ref, wye_ref, wyp_ref,
    x_ref, veco_ref,
    upo_ref, upp_ref, dno_ref, dnp_ref,
    xhat_ref, rstd_ref, low_ref, acto_ref, actp_ref, dgo_ref, dgp_ref, part_ref,
):
    span = slice(chunk * HALF, (chunk + 1) * HALF)
    base = pl.multiple_of(base_ref[0] + chunk * HALF, HALF)
    mine = dot(co_ref[:, span], wo_ref[...], 0, 0) + dot(cp_ref[:, span], wp_ref[...], 0, 0)
    peer = dot(eo_ref[:, span], wye_ref[...], 0, 0) + dot(ep_ref[:, span], wyp_ref[...], 0, 0)
    attn = mine.astype(BF).astype(F32) + peer.astype(BF).astype(F32)
    vec = veco_ref[...].astype(F32)
    mixed = x_ref[pl.ds(base, HALF), :].astype(F32) + attn + vec[B_OUT : B_OUT + 1]
    mean = jnp.mean(mixed, axis=-1, keepdims=True)
    centred = mixed - mean
    rstd = lax.rsqrt(jnp.mean(centred * centred, axis=-1, keepdims=True) + NORM_EPS)
    xhat = centred * rstd
    xhat_ref[...] = xhat
    rstd_ref[...] = rstd
    low = (xhat * vec[GAIN1 : GAIN1 + 1] + vec[SHIFT1 : SHIFT1 + 1]).astype(BF)
    low_ref[...] = low
    down = None
    for up_ref, dn_ref, bias, act_ref, dg_ref in (
        (upo_ref, dno_ref, vec[B_UP : B_UP + 1], acto_ref, dgo_ref),
        (upp_ref, dnp_ref, vec[B_UP_P : B_UP_P + 1], actp_ref, dgp_ref),
    ):
        hidden = dot(low, up_ref[...], 1, 0) + bias
        phi = 0.5 + 0.5 * lax.erf(hidden * (0.5**0.5))
        dens = jnp.exp(hidden * hidden * -0.5) * (0.5 * 2.0**0.5 / jnp.pi**0.5)
        act = (hidden * phi).astype(BF)
        act_ref[...] = act
        dg_ref[...] = (phi + hidden * dens).astype(BF)
        term = dot(act, dn_ref[...], 1, 0)
        down = term if down is None else down + term
    part_ref[...] = down.astype(BF)


def ffn(chunk, base, ctxs, wouts, x, veco, ups, downs):
    d = x.shape[1]
    f = ups[0].shape[1]
    rows = HALF
    return vmem_call(
        partial(ffn_kernel, chunk),
        [((rows, d), F32), ((rows, 1), F32), ((rows, d), BF)]
        + [((rows, f), BF)] * 4
        + [((rows, d), BF)],
        [base],
        [*ctxs, *wouts, x, veco, *ups, *downs],
    )


def back_kernel(
    chunk,
    base_ref,
    mine_ref, peer_ref, xhat_ref, vec_ref, grad_ref,
    dgo_ref, dgp_ref, upo_ref, upp_ref, dno_ref, dnp_ref,
    out_ref, dsec_ref, dlow_ref, dho_ref, dhp_ref, part_ref, sums_ref,
):
    base = pl.multiple_of(base_ref[0] + chunk * HALF, HALF)
    vec = vec_ref[...].astype(F32)
    normed = xhat_ref[...] * vec[GAIN1 : GAIN1 + 1] + vec[SHIFT1 : SHIFT1 + 1]
    total = mine_ref[...].astype(F32) + peer_ref[...].astype(F32)
    second = normed + total + vec[B_DOWN : B_DOWN + 1]
    mean = jnp.mean(second, axis=-1, keepdims=True)
    centred = second - mean
    rstd = lax.rsqrt(jnp.mean(centred * centred, axis=-1, keepdims=True) + NORM_EPS)
    xhat = centred * rstd
    gain = vec[GAIN2 : GAIN2 + 1]
    out_ref[...] = (xhat * gain + vec[SHIFT2 : SHIFT2 + 1]).astype(BF)
    grad = grad_ref[pl.ds(base, HALF), :].astype(F32)
    scaled = grad * gain
    dsec = rstd * (
        scaled
        - jnp.mean(scaled, axis=-1, keepdims=True)
        - xhat * jnp.mean(scaled * xhat, axis=-1, keepdims=True)
    )
    dsec_ref[...] = dsec
    dlow = dsec.astype(BF)
    dlow_ref[...] = dlow
    sums_ref[...] = jnp.zeros_like(sums_ref)
    sums_ref[0:1] = jnp.sum(grad * xhat, axis=0, keepdims=True)
    sums_ref[1:2] = jnp.sum(grad, axis=0, keepdims=True)
    sums_ref[2:3] = jnp.sum(dsec, axis=0, keepdims=True)
    part = None
    for k, (up_ref, dn_ref, dg_ref, dh_ref) in enumerate(
        ((upo_ref, dno_ref, dgo_ref, dho_ref), (upp_ref, dnp_ref, dgp_ref, dhp_ref))
    ):
        dh = dot(dlow, dn_ref[...], 1, 1) * dg_ref[...].astype(F32)
        sums_ref[3 + k : 4 + k] = jnp.sum(dh, axis=0, keepdims=True)
        dh = dh.astype(BF)
        dh_ref[...] = dh
        term = dot(dh, up_ref[...], 1, 1)
        part = term if part is None else part + term
    part_ref[...] = part.astype(BF)


def back(chunk, base, mine, peer, xhat, vec, grad, dgs, ups, downs):
    rows, d = xhat.shape
    f = ups[0].shape[1]
    return vmem_call(
        partial(back_kernel, chunk),
        [((rows, d), BF), ((rows, d), F32), ((rows, d), BF), ((rows, f), BF), ((rows, f), BF)]
        + [((rows, d), BF), ((8, d), F32)],
        [base],
        [mine, peer, xhat, vec, grad, *dgs, *ups, *downs],
        pace=PACE // (1 + 9 * chunk),
    )


def wgrad_kernel(base_ref, la_ref, lb_ref, ra_ref, rb_ref, out_ref):
    total = dot(la_ref[...], ra_ref[...], 0, 0) + dot(lb_ref[...], rb_ref[...], 0, 0)
    out_ref[...] = total.astype(BF)


def wgrad(base, lefts, rights):
    rows, a = lefts[0].shape
    b = rights[0].shape[1]
    return vmem_call(
        wgrad_kernel, [((a, b), BF)], [base], [*lefts, *rights]
    )[0]


def mix_kernel(
    base_ref,
    dsec_ref, mine_ref, peer_ref, xhat_ref, rstd_ref, vec_ref, wo_ref, wp_ref,
    dmix_ref, dlow_ref, dco_ref, dcp_ref, sums_ref,
):
    gain = vec_ref[GAIN1 : GAIN1 + 1].astype(F32)
    grad = mine_ref[...].astype(F32) + peer_ref[...].astype(F32) + dsec_ref[...]
    xhat = xhat_ref[...]
    scaled = grad * gain
    dmix = rstd_ref[...] * (
        scaled
        - jnp.mean(scaled, axis=-1, keepdims=True)
        - xhat * jnp.mean(scaled * xhat, axis=-1, keepdims=True)
    )
    dmix_ref[...] = dmix
    low = dmix.astype(BF)
    dlow_ref[...] = low
    sums_ref[...] = jnp.zeros_like(sums_ref)
    sums_ref[0:1] = jnp.sum(grad * xhat, axis=0, keepdims=True)
    sums_ref[1:2] = jnp.sum(grad, axis=0, keepdims=True)
    sums_ref[2:3] = jnp.sum(dmix, axis=0, keepdims=True)
    dco_ref[...] = dot(wo_ref[...], low, 1, 1).astype(BF)
    dcp_ref[...] = dot(wp_ref[...], low, 1, 1).astype(BF)


def mix_back(base, dsec, mine, peer, xhat, rstd, vec, wouts):
    rows, d = xhat.shape
    cols = wouts[0].shape[0]
    return vmem_call(
        mix_kernel,
        [((rows, d), F32), ((rows, d), BF), ((cols, rows), BF), ((cols, rows), BF), ((8, d), F32)],
        [base],
        [dsec, mine, peer, xhat, rstd, vec, *wouts],
    )


def attend_back_kernel(
    own,
    base_ref,
    qkv_ref, p_ref, ctx_ref, dca_ref, dcb_ref, x_ref, w_ref, dla_ref, dlb_ref,
    s1a_ref, s1b_ref, s2a_ref, s2b_ref, *rest
):
    given_ref = rest[0] if len(rest) == 5 else None
    gw_ref, part_ref, tail_ref, d_ref = rest[-4:]
    cols = ctx_ref.shape[0]
    base = pl.multiple_of(base_ref[0], SEG)
    for h in range(cols // HEAD):
        at = h * HEAD
        query = qkv_ref[at : at + HEAD, :]
        key = qkv_ref[cols + at : cols + at + HEAD, :]
        value = qkv_ref[2 * cols + at : 2 * cols + at + HEAD, :]
        d_ctx = jnp.concatenate([dca_ref[at : at + HEAD, :], dcb_ref[at : at + HEAD, :]], axis=1)
        probs = p_ref[h]
        inner = jnp.sum(
            d_ctx.astype(F32) * ctx_ref[at : at + HEAD, :].astype(F32), axis=0, keepdims=True
        )
        d_probs = dot(value, d_ctx, 0, 0)
        d_scores = (probs.astype(F32) * (d_probs - inner)).astype(BF)
        scale = HEAD**-0.5
        d_ref[at : at + HEAD, :] = (dot(key, d_scores, 1, 0) * scale).astype(BF)
        d_ref[cols + at : cols + at + HEAD, :] = (dot(query, d_scores, 1, 1) * scale).astype(BF)
        d_ref[2 * cols + at : 2 * cols + at + HEAD, :] = dot(d_ctx, probs, 1, 1).astype(BF)
    part = dot(d_ref[...], w_ref[...], 0, 0)
    if given_ref is None:
        part_ref[...] = part
    else:
        part_ref[...] = (part + given_ref[...]).astype(BF)
    gw_ref[0:cols, :] = (
        dot(ctx_ref[:, 0:HALF], dla_ref[...], 1, 0) + dot(ctx_ref[:, HALF:], dlb_ref[...], 1, 0)
    ).astype(BF)
    gw_ref[cols : 4 * cols, :] = dot(d_ref[...], x_ref[pl.ds(base, SEG), :], 1, 0).astype(BF)
    ones = jnp.ones((16, SEG), BF)
    tail_ref[...] = jnp.zeros_like(tail_ref)
    s1 = s1a_ref[...] + s1b_ref[...]
    s2 = s2a_ref[...] + s2b_ref[...]
    tail_ref[B_OUT : B_OUT + 1] = s1[2:3]
    tail_ref[GAIN1 : SHIFT1 + 1] = s1[0:2]
    tail_ref[B_DOWN : B_DOWN + 1] = s2[2:3]
    tail_ref[GAIN2 : SHIFT2 + 1] = s2[0:2]
    tail_ref[B_UP : B_UP + 1] = s2[3:4] if own else s2[4:5]
    tail_ref[B_QV : B_QV + 1, 0:cols] = dot(ones, d_ref[0:cols, :], 1, 1)[0:1]
    tail_ref[B_QV : B_QV + 1, V_AT : V_AT + cols] = dot(ones, d_ref[2 * cols :, :], 1, 1)[0:1]
    gw_ref[4 * cols :, :] = tail_ref[...].astype(BF)


def attend_back(own, base, qkv, probs, ctx, dctx, x, w, dlow, sums1, sums2, given=None):
    cols, seg = ctx.shape
    d = x.shape[1]
    arrays = [qkv, probs, ctx, *dctx, x, w, *dlow, *sums1, *sums2]
    if given is not None:
        arrays.append(given)
    return vmem_call(
        partial(attend_back_kernel, own),
        [((4 * cols + TAIL, d), BF), ((seg, d), F32 if given is None else BF)],
        [base],
        arrays,
        scratch=[pltpu.VMEM((TAIL, d), F32), pltpu.VMEM((3 * cols, seg), BF)],
    )


def grad_kernel(base_ref, dma_ref, dmb_ref, mine_ref, peer_ref, out_ref):
    total = mine_ref[...].astype(F32) + peer_ref[...].astype(F32)
    out_ref[0:HALF] = (dma_ref[...] + total[0:HALF]).astype(BF)
    out_ref[HALF:] = (dmb_ref[...] + total[HALF:]).astype(BF)


def place_kernel(base_ref, *refs):
    out_ref = refs[-1]
    each = len(refs) // 2
    own = pl.multiple_of(base_ref[0], SEG)
    other = pl.multiple_of(SEG - base_ref[0], SEG)
    at = 0
    for mine_ref, came_ref in zip(refs[:each], refs[each:-1]):
        rows = mine_ref.shape[0]
        out_ref[pl.ds(own + at, rows), :] = mine_ref[...]
        out_ref[pl.ds(other + at, rows), :] = came_ref[...]
        at += rows


def place(base, own, came):
    return vmem_call(
        place_kernel, [((2 * SEG, own[0].shape[1]), BF)], [base], [*own, *came]
    )[0]


X, Z0, Z1 = range(3)


def hop(array, size, bit):
    return lax.ppermute(array, "dp", [(i, i ^ (1 << bit)) for i in range(size)])


def add_kernel(bit_ref, mine_ref, came_ref, *refs):
    total = mine_ref[...].astype(F32) + came_ref[...].astype(F32)
    if len(refs) == 1:
        refs[0][...] = total.astype(BF)
        return
    keep_ref, send_ref, total_ref = refs
    rows = keep_ref.shape[0]
    total_ref[...] = total.astype(BF)
    keep_ref[...] = total_ref[pl.ds(pl.multiple_of(bit_ref[0] * rows, 8), rows), :]
    send_ref[...] = total_ref[pl.ds(pl.multiple_of((1 - bit_ref[0]) * rows, 8), rows), :]


def add(bit, mine, came, halves):
    rows, d = mine.shape
    if not halves:
        return vmem_call(add_kernel, [((rows, d), BF)], [bit], [mine, came], limit=8)[0]
    return vmem_call(
        add_kernel, [((rows // 2, d), BF)] * 2, [bit], [mine, came], limit=8,
        scratch=[pltpu.VMEM((rows, d), BF)],
    )


def join_kernel(spans, bit_ref, mine_ref, came_ref, *refs):
    both_ref = refs[-1] if len(refs) > len(spans) else refs[0]
    rows = mine_ref.shape[0]
    own = pl.multiple_of(bit_ref[0] * rows, 8)
    other = pl.multiple_of((1 - bit_ref[0]) * rows, 8)
    both_ref[pl.ds(own, rows), :] = mine_ref[...].astype(both_ref.dtype)
    both_ref[pl.ds(other, rows), :] = came_ref[...].astype(both_ref.dtype)
    if len(refs) > len(spans):
        at = 0
        for ref, span in zip(refs, spans):
            ref[...] = both_ref[at : at + span, :].astype(ref.dtype)
            at += span


def join(bit, mine, came, spans, dtype):
    rows, d = mine.shape
    scratch = [] if len(spans) == 1 else [pltpu.VMEM((2 * rows, d), BF)]
    return vmem_call(
        partial(join_kernel, spans), [((span, d), dtype) for span in spans], [bit], [mine, came],
        limit=8, scratch=scratch,
    )


class Line:
    def __init__(self):
        self.last = None

    def at(self, value):
        return value if self.last is None else after(value, self.last)

    def done(self, value):
        self.last = value
        return value


def reduce_dp(line, mine, came, size, spans, order=(X, Z0, Z1)):
    if size != 8:
        rows = mine.shape[0]
        total = lax.psum((mine.astype(F32) + came.astype(F32)).astype(BF), "dp").astype(F32)
        for _ in range(6):
            yield None
        ends = [sum(spans[: k + 1]) for k in range(len(spans))]
        yield [total[e - n : e] for e, n in zip(ends, spans)]
        return
    place_in = lax.axis_index("dp")
    bits = [jnp.reshape((place_in >> k) & 1, (1,)).astype(jnp.int32) for k in range(3)]
    for bit in order:
        mine, send = add(line.at(bits[bit]), mine, came, True)
        line.done(send)
        came = hop(send, size, bit)
        yield None
    mine = line.done(add(line.at(bits[order[0]]), mine, came, False))
    for bit in order[::-1]:
        came = hop(mine, size, bit)
        yield None
        last = bit == order[0]
        parts = join(line.at(bits[bit]), mine, came, spans if last else (2 * mine.shape[0],),
                     F32 if last else BF)
        mine = line.done(parts[0])
    yield parts


def shards(dp_size, tensor_size, seg_input, w_qkv, b_qv, w_out, b_out, norm1_gain, norm1_bias,
           w_up, b_up, w_down, b_down, norm2_gain, norm2_bias, doc_ids, mem_live, out_grad):
    d = seg_input.shape[1]
    cols = w_qkv.shape[2]
    place_in = lax.axis_index("tensor")
    core = place_in % 2
    base = jnp.reshape(core * SEG, (1,)).astype(jnp.int32)
    near = [(i, i ^ 1) for i in range(tensor_size)]
    far = [(i, i ^ 2) for i in range(tensor_size)]

    def to_core(a):
        return lax.ppermute(a, "tensor", near)

    def to_peer(a):
        return lax.ppermute(a, "tensor", far)

    spot = jnp.arange(SEG, dtype=jnp.int32)[None]
    token = (spot >= MEM) & (spot < MEM + SEGTOK)
    dead = (spot < MEM) & (spot >= mem_live[:, None])
    padded = jnp.pad(doc_ids, ((0, 0), (MEM, SEG - MEM - SEGTOK)))
    codes = jnp.where(token, padded, jnp.where(dead, -2, -1)).astype(BF)
    bias_o = jnp.concatenate([b_qv, b_up.reshape(d // cols, cols),
                              jnp.zeros((BIAS_ROWS - 2 - d // cols, cols), BF)])

    line = Line()

    def now():
        return line.at(base)

    w_o = jnp.transpose(w_qkv, (1, 2, 0)).reshape(3 * cols, d)
    bias_p = to_core(bias_o)
    w_p = to_core(w_o)
    wout_e = to_peer(w_out)
    up_p = to_core(w_up)
    down_p = to_core(w_down)
    ups, downs = (w_up, up_p), (w_down, down_p)

    ctx_o, probs_o, qkv_o = attend(base, codes, seg_input, w_o, bias_o)
    line.done(ctx_o)
    ctx_eo = to_peer(ctx_o)
    wout_p = to_core(line.at(w_out))
    ctx_p, probs_p, qkv_p = attend(after(now(), up_p, down_p), codes, seg_input, w_p, bias_p)
    line.done(ctx_p)
    ctx_ep = to_peer(ctx_p)
    wout_ep = to_core(wout_e)
    b_up_p = bias_p[2 : 2 + d // cols].reshape(d)
    row = jnp.arange(8, dtype=jnp.int32)[:, None]
    vec = jnp.broadcast_to(b_up_p, (8, d))
    for k, one in enumerate((b_out, norm1_gain, norm1_bias, b_down, norm2_gain, norm2_bias, b_up)):
        vec = jnp.where(row == k, one, vec)
    fwd = []
    for k in range(2):
        fwd.append(ffn(k, now(), (ctx_o, ctx_p, ctx_eo, ctx_ep), (w_out, wout_p, wout_e, wout_ep),
                       seg_input, vec, ups, downs))
        line.done(fwd[-1][-1])
    xhat, rstd, low, act_o, act_p, dg_o, dg_p, part = zip(*fwd)
    peer = [to_peer(p) for p in part]
    bwd = []
    for k in range(2):
        bwd.append(back(k, now(), part[k], peer[k], xhat[k], vec, out_grad, (dg_o[k], dg_p[k]),
                        ups, downs))
        line.done(bwd[-1][-2])
    out, dsec, dlow, dh_o, dh_p, npart, sums2 = zip(*bwd)
    npeer = [to_peer(p) for p in npart]
    gdown_p = to_core(line.done(wgrad(now(), act_p, dlow)))
    gup_p = to_core(line.done(wgrad(now(), low, dh_p)))
    gdown = line.done(wgrad(now(), act_o, dlow))
    gup = line.done(wgrad(now(), low, dh_o))
    chains = {
        "D": reduce_dp(line, gdown, gdown_p, dp_size, gdown.shape[:1]),
        "U": reduce_dp(line, gup, gup_p, dp_size, gup.shape[:1], (Z0, Z1, X)),
    }
    sums = {}

    def go(names):
        for name in names:
            sums[name] = next(chains[name])

    mixes = []
    for k in range(2):
        mixes.append(mix_back(now(), dsec[k], npart[k], npeer[k], xhat[k], rstd[k], vec,
                              (w_out, wout_p)))
        line.done(mixes[-1][1])
        if k == 0:
            go("DU")
    dmix, dmlow, dc_o, dc_p, sums1 = zip(*mixes)
    gw_p, ipart = attend_back(False, now(), qkv_p, probs_p, ctx_p, dc_p, seg_input, w_p, dmlow,
                              sums1, sums2)
    line.done(gw_p)
    gw_p = to_core(gw_p)
    gw_o, ipart = attend_back(True, now(), qkv_o, probs_o, ctx_o, dc_o, seg_input, w_o, dmlow,
                              sums1, sums2, ipart)
    line.done(gw_o)
    ipeer = to_peer(ipart)
    chains["R"] = reduce_dp(line, gw_o, gw_p, dp_size, (cols, 3 * cols, TAIL))
    go("DURD")
    own_grad = line.done(vmem_call(grad_kernel, [((SEG, d), BF)], [now()],
                                   [*dmix, ipart, ipeer])[0])
    own_came = to_core(own_grad)
    go("RUD")
    grad_input = line.done(place(now(), [own_grad], [own_came]))
    go("R")
    out_came = [to_core(line.at(o)) for o in out]
    go("DURU")
    seg_output = line.done(place(now(), out, out_came))
    go("DRRUDRU")

    (grad_w_down,), (grad_w_up,), (grad_w_out, grad_qkv, tail) = (sums[k] for k in "DUR")

    grad_w_qkv = jnp.transpose(grad_qkv.reshape(3, cols, d), (2, 0, 1))
    grad_b_qv = jnp.stack([tail[B_QV, 0:cols], tail[B_QV, V_AT : V_AT + cols]])
    return (seg_output, grad_input, grad_w_qkv, grad_b_qv, grad_w_out, tail[B_OUT], tail[GAIN1],
            tail[SHIFT1], grad_w_up, tail[B_UP], grad_w_down, tail[B_DOWN], tail[GAIN2],
            tail[SHIFT2])


def solution(mesh):
    wide, col, row, one = P("dp", None), P(None, "tensor"), P("tensor", None), P()
    return jax.shard_map(
        partial(shards, mesh.shape["dp"], mesh.shape["tensor"]),
        mesh=mesh,
        in_specs=(wide, P(None, None, "tensor"), col, row, one, one, one, col, P("tensor"), row,
                  one, one, one, wide, P("dp"), wide),
        out_specs=(wide, wide, P(None, None, "tensor"), col, row, one, one, one, col, P("tensor"),
                   row, one, one, one),
        check_vma=False,
    )
```

```python
from functools import partial

import jax
import jax.numpy as jnp
import numpy as np
from jax import lax
from jax.experimental import pallas as pl
from jax.experimental.pallas import tpu as pltpu
from jax.sharding import PartitionSpec as P

HEAD = 64
MEM = 10
SEGTOK = 492
SEG = 512
HALF = 256
MASKED_SCORE = -1e30
NORM_EPS = 1e-05
BF = jnp.bfloat16
F32 = jnp.float32
B_OUT, GAIN1, SHIFT1, B_DOWN, GAIN2, SHIFT2, B_UP, B_QV = range(8)
TAIL = 64
PACE = 10_000_000_000
V_AT = 256


def dot(left, right, left_dim, right_dim):
    return lax.dot_general(
        left, right, (((left_dim,), (right_dim,)), ((), ())), preferred_element_type=F32
    )


def after(value, *earlier):
    return lax.optimization_barrier((value, *earlier))[0]


def vmem_call(body, outs, scalars, arrays, scratch=(), limit=16, pace=PACE, far_outs=()):
    near = pl.BlockSpec(memory_space=pltpu.VMEM)
    return pl.pallas_call(
        body,
        out_shape=[jax.ShapeDtypeStruct(s, d) for s, d in outs]
        + [pltpu.HBM(s, d) for s, d in far_outs],
        in_specs=[pl.BlockSpec(memory_space=pltpu.SMEM)] * len(scalars) + [near] * len(arrays),
        out_specs=[near] * len(outs) + [pl.BlockSpec(memory_space=pltpu.HBM)] * len(far_outs),
        scratch_shapes=list(scratch),
        compiler_params=pltpu.CompilerParams(vmem_limit_bytes=limit << 20),
        cost_estimate=pl.CostEstimate(flops=pace, bytes_accessed=0, transcendentals=0),
    )(*scalars, *arrays)


def attend_kernel(base_ref, codes_ref, x_ref, w_ref, bias_ref, ctx_ref, *refs):
    p_ref, qkv_ref, mask_ref = refs[-4:-1] if len(refs) == 6 else refs
    cols = ctx_ref.shape[0]
    heads = cols // HEAD
    core = base_ref[0] // SEG
    proj = dot(w_ref[...], x_ref[...], 1, 1)
    line = lax.broadcasted_iota(jnp.int32, (8, SEG), 0)
    b_query = dot(bias_ref[:, 0:cols], (line == 1).astype(BF), 0, 0)
    b_value = dot(bias_ref[:, 0:cols], (line == 2).astype(BF), 0, 0)
    qkv_ref[0:cols, :] = (proj[0:cols] + b_query).astype(BF)
    qkv_ref[cols : 2 * cols, :] = proj[cols : 2 * cols].astype(BF)
    qkv_ref[2 * cols :, :] = (proj[2 * cols :] + b_value).astype(BF)
    codes = codes_ref[...].astype(F32)
    key_line = jnp.where(core == 0, codes[0:1], codes[1:2])
    spot = lax.broadcasted_iota(jnp.int32, (1, SEG), 1)
    token = (spot >= MEM) & (spot < MEM + SEGTOK)
    query_code = jnp.where(token, key_line, 99.0)
    first = (lax.broadcasted_iota(jnp.int32, (16, SEG), 0) == 0).astype(BF)
    key_code = dot(jnp.broadcast_to(key_line, (16, SEG)).astype(BF), first, 0, 0)
    allowed = (key_code == query_code) | (key_code == -1.0)
    allowed = allowed | ((query_code == 99.0) & (key_code >= 0.0))
    mask_ref[...] = jnp.where(allowed, 0.0, MASKED_SCORE)
    for h in range(heads):
        at = h * HEAD
        query = qkv_ref[at : at + HEAD, :] * BF(HEAD**-0.5)
        key = qkv_ref[cols + at : cols + at + HEAD, :]
        value = qkv_ref[2 * cols + at : 2 * cols + at + HEAD, :]
        scores = dot(key, query, 0, 0) + mask_ref[...]
        top = jnp.max(scores, axis=0, keepdims=True)
        exps = jnp.exp(scores - top)
        total = jnp.sum(exps, axis=0, keepdims=True)
        probs = (exps * (1.0 / total)).astype(BF)
        p_ref[h] = probs
        ctx_ref[at : at + HEAD, :] = dot(value, probs, 1, 0).astype(BF)
    if len(refs) == 6:
        sems = refs[-1]
        copies = [pltpu.make_async_copy(p_ref, refs[0], sems.at[0]),
                  pltpu.make_async_copy(qkv_ref, refs[1], sems.at[1])]
        for copy in copies:
            copy.start()
        for copy in copies:
            copy.wait()


def attend(base, codes, x, w, bias, far):
    cols = w.shape[0] // 3
    heads = cols // HEAD
    saved = [((heads, SEG, SEG), BF), ((3 * cols, SEG), BF)]
    scratch = [pltpu.VMEM((SEG, SEG), F32)]
    if far:
        scratch = [pltpu.VMEM(*one) for one in saved] + scratch + [pltpu.SemaphoreType.DMA((2,))]
    return vmem_call(
        attend_kernel,
        [((cols, SEG), BF)] + ([] if far else saved),
        [base],
        [codes, x, w, bias],
        scratch=scratch,
        far_outs=saved if far else (),
    )


def ffn_kernel(
    chunk,
    base_ref,
    co_ref, cp_ref, eo_ref, ep_ref,
    wo_ref, wp_ref, wye_ref, wyp_ref,
    x_ref, veco_ref, vecp_ref,
    upo_ref, upp_ref, dno_ref, dnp_ref,
    xhat_ref, rstd_ref, low_ref, acto_ref, actp_ref, dgo_ref, dgp_ref, part_ref,
):
    span = slice(chunk * HALF, (chunk + 1) * HALF)
    mine = dot(co_ref[:, span], wo_ref[...], 0, 0) + dot(cp_ref[:, span], wp_ref[...], 0, 0)
    peer = dot(eo_ref[:, span], wye_ref[...], 0, 0) + dot(ep_ref[:, span], wyp_ref[...], 0, 0)
    attn = mine.astype(BF).astype(F32) + peer.astype(BF).astype(F32)
    vec = veco_ref[...].astype(F32)
    mixed = x_ref[span, :].astype(F32) + attn + vec[B_OUT : B_OUT + 1]
    mean = jnp.mean(mixed, axis=-1, keepdims=True)
    centred = mixed - mean
    rstd = lax.rsqrt(jnp.mean(centred * centred, axis=-1, keepdims=True) + NORM_EPS)
    xhat = centred * rstd
    xhat_ref[...] = xhat
    rstd_ref[...] = rstd
    low = (xhat * vec[GAIN1 : GAIN1 + 1] + vec[SHIFT1 : SHIFT1 + 1]).astype(BF)
    low_ref[...] = low
    down = None
    for up_ref, dn_ref, bias, act_ref, dg_ref in (
        (upo_ref, dno_ref, vec[B_UP : B_UP + 1], acto_ref, dgo_ref),
        (upp_ref, dnp_ref, vecp_ref[...].astype(F32)[0:1], actp_ref, dgp_ref),
    ):
        hidden = dot(low, up_ref[...], 1, 0) + bias
        phi = 0.5 + 0.5 * lax.erf(hidden * (0.5**0.5))
        dens = jnp.exp(hidden * hidden * -0.5) * (0.5 * 2.0**0.5 / jnp.pi**0.5)
        act = (hidden * phi).astype(BF)
        act_ref[...] = act
        dg_ref[...] = (phi + hidden * dens).astype(BF)
        term = dot(act, dn_ref[...], 1, 0)
        down = term if down is None else down + term
    part_ref[...] = down.astype(BF)


def ffn(chunk, base, ctxs, wouts, x, veco, vecp, ups, downs):
    d = x.shape[1]
    f = ups[0].shape[1]
    rows = HALF
    return vmem_call(
        partial(ffn_kernel, chunk),
        [((rows, d), F32), ((rows, 1), F32), ((rows, d), BF)]
        + [((rows, f), BF)] * 4
        + [((rows, d), BF)],
        [base],
        [*ctxs, *wouts, x, veco, vecp, *ups, *downs],
    )


def back_kernel(
    chunk,
    base_ref,
    mine_ref, peer_ref, xhat_ref, vec_ref, grad_ref,
    dgo_ref, dgp_ref, upo_ref, upp_ref, dno_ref, dnp_ref,
    out_ref, dsec_ref, dlow_ref, dho_ref, dhp_ref, part_ref, sums_ref,
):
    base = pl.multiple_of(base_ref[0] + chunk * HALF, HALF)
    vec = vec_ref[...].astype(F32)
    normed = xhat_ref[...] * vec[GAIN1 : GAIN1 + 1] + vec[SHIFT1 : SHIFT1 + 1]
    total = mine_ref[...].astype(F32) + peer_ref[...].astype(F32)
    second = normed + total + vec[B_DOWN : B_DOWN + 1]
    mean = jnp.mean(second, axis=-1, keepdims=True)
    centred = second - mean
    rstd = lax.rsqrt(jnp.mean(centred * centred, axis=-1, keepdims=True) + NORM_EPS)
    xhat = centred * rstd
    gain = vec[GAIN2 : GAIN2 + 1]
    out_ref[...] = (xhat * gain + vec[SHIFT2 : SHIFT2 + 1]).astype(BF)
    grad = grad_ref[pl.ds(base, HALF), :].astype(F32)
    scaled = grad * gain
    dsec = rstd * (
        scaled
        - jnp.mean(scaled, axis=-1, keepdims=True)
        - xhat * jnp.mean(scaled * xhat, axis=-1, keepdims=True)
    )
    dsec_ref[...] = dsec
    dlow = dsec.astype(BF)
    dlow_ref[...] = dlow
    sums_ref[...] = jnp.zeros_like(sums_ref)
    sums_ref[0:1] = jnp.sum(grad * xhat, axis=0, keepdims=True)
    sums_ref[1:2] = jnp.sum(grad, axis=0, keepdims=True)
    sums_ref[2:3] = jnp.sum(dsec, axis=0, keepdims=True)
    part = None
    for k, (up_ref, dn_ref, dg_ref, dh_ref) in enumerate(
        ((upo_ref, dno_ref, dgo_ref, dho_ref), (upp_ref, dnp_ref, dgp_ref, dhp_ref))
    ):
        dh = dot(dlow, dn_ref[...], 1, 1) * dg_ref[...].astype(F32)
        sums_ref[3 + k : 4 + k] = jnp.sum(dh, axis=0, keepdims=True)
        dh = dh.astype(BF)
        dh_ref[...] = dh
        term = dot(dh, up_ref[...], 1, 1)
        part = term if part is None else part + term
    part_ref[...] = part.astype(BF)


def back(chunk, base, mine, peer, xhat, vec, grad, dgs, ups, downs):
    rows, d = xhat.shape
    f = ups[0].shape[1]
    return vmem_call(
        partial(back_kernel, chunk),
        [((rows, d), BF), ((rows, d), F32), ((rows, d), BF), ((rows, f), BF), ((rows, f), BF)]
        + [((rows, d), BF), ((8, d), F32)],
        [base],
        [mine, peer, xhat, vec, grad, *dgs, *ups, *downs],
        pace=PACE // (1 + 9 * chunk),
    )


def wgrad_kernel(base_ref, la_ref, lb_ref, ra_ref, rb_ref, out_ref):
    total = dot(la_ref[...], ra_ref[...], 0, 0) + dot(lb_ref[...], rb_ref[...], 0, 0)
    out_ref[...] = total.astype(BF)


def wgrad(base, lefts, rights):
    rows, a = lefts[0].shape
    b = rights[0].shape[1]
    return vmem_call(
        wgrad_kernel, [((a, b), BF)], [base], [*lefts, *rights]
    )[0]


def mix_kernel(
    base_ref,
    dsec_ref, mine_ref, peer_ref, xhat_ref, rstd_ref, vec_ref, wo_ref, wp_ref,
    dmix_ref, dlow_ref, dco_ref, dcp_ref, sums_ref,
):
    gain = vec_ref[GAIN1 : GAIN1 + 1].astype(F32)
    grad = mine_ref[...].astype(F32) + peer_ref[...].astype(F32) + dsec_ref[...]
    xhat = xhat_ref[...]
    scaled = grad * gain
    dmix = rstd_ref[...] * (
        scaled
        - jnp.mean(scaled, axis=-1, keepdims=True)
        - xhat * jnp.mean(scaled * xhat, axis=-1, keepdims=True)
    )
    dmix_ref[...] = dmix
    low = dmix.astype(BF)
    dlow_ref[...] = low
    sums_ref[...] = jnp.zeros_like(sums_ref)
    sums_ref[0:1] = jnp.sum(grad * xhat, axis=0, keepdims=True)
    sums_ref[1:2] = jnp.sum(grad, axis=0, keepdims=True)
    sums_ref[2:3] = jnp.sum(dmix, axis=0, keepdims=True)
    dco_ref[...] = dot(wo_ref[...], low, 1, 1).astype(BF)
    dcp_ref[...] = dot(wp_ref[...], low, 1, 1).astype(BF)


def mix_back(base, dsec, mine, peer, xhat, rstd, vec, wouts):
    rows, d = xhat.shape
    cols = wouts[0].shape[0]
    return vmem_call(
        mix_kernel,
        [((rows, d), F32), ((rows, d), BF), ((cols, rows), BF), ((cols, rows), BF), ((8, d), F32)],
        [base],
        [dsec, mine, peer, xhat, rstd, vec, *wouts],
    )


def attend_back_kernel(
    own,
    base_ref,
    qkv_ref, p_ref, ctx_ref, dca_ref, dcb_ref, x_ref, w_ref, dla_ref, dlb_ref,
    s1a_ref, s1b_ref, s2a_ref, s2b_ref, *rest
):
    given_ref = rest[0] if len(rest) == 5 else None
    gw_ref, part_ref, tail_ref, d_ref = rest[-4:]
    cols = ctx_ref.shape[0]
    for h in range(cols // HEAD):
        at = h * HEAD
        query = qkv_ref[at : at + HEAD, :]
        key = qkv_ref[cols + at : cols + at + HEAD, :]
        value = qkv_ref[2 * cols + at : 2 * cols + at + HEAD, :]
        d_ctx = jnp.concatenate([dca_ref[at : at + HEAD, :], dcb_ref[at : at + HEAD, :]], axis=1)
        probs = p_ref[h]
        inner = jnp.sum(
            d_ctx.astype(F32) * ctx_ref[at : at + HEAD, :].astype(F32), axis=0, keepdims=True
        )
        d_probs = dot(value, d_ctx, 0, 0)
        d_scores = (probs.astype(F32) * (d_probs - inner)).astype(BF)
        scale = HEAD**-0.5
        d_ref[at : at + HEAD, :] = (dot(key, d_scores, 1, 0) * scale).astype(BF)
        d_ref[cols + at : cols + at + HEAD, :] = (dot(query, d_scores, 1, 1) * scale).astype(BF)
        d_ref[2 * cols + at : 2 * cols + at + HEAD, :] = dot(d_ctx, probs, 1, 1).astype(BF)
    part = dot(d_ref[...], w_ref[...], 0, 0)
    if given_ref is None:
        part_ref[...] = part
    else:
        part_ref[...] = (part + given_ref[...]).astype(BF)
    gw_ref[0:cols, :] = (
        dot(ctx_ref[:, 0:HALF], dla_ref[...], 1, 0) + dot(ctx_ref[:, HALF:], dlb_ref[...], 1, 0)
    ).astype(BF)
    gw_ref[cols : 4 * cols, :] = dot(d_ref[...], x_ref[...], 1, 0).astype(BF)
    ones = jnp.ones((16, SEG), BF)
    tail_ref[...] = jnp.zeros_like(tail_ref)
    s1 = s1a_ref[...] + s1b_ref[...]
    s2 = s2a_ref[...] + s2b_ref[...]
    tail_ref[B_OUT : B_OUT + 1] = s1[2:3]
    tail_ref[GAIN1 : SHIFT1 + 1] = s1[0:2]
    tail_ref[B_DOWN : B_DOWN + 1] = s2[2:3]
    tail_ref[GAIN2 : SHIFT2 + 1] = s2[0:2]
    tail_ref[B_UP : B_UP + 1] = s2[3:4] if own else s2[4:5]
    tail_ref[B_QV : B_QV + 1, 0:cols] = dot(ones, d_ref[0:cols, :], 1, 1)[0:1]
    tail_ref[B_QV : B_QV + 1, V_AT : V_AT + cols] = dot(ones, d_ref[2 * cols :, :], 1, 1)[0:1]
    gw_ref[4 * cols :, :] = tail_ref[...].astype(BF)


def attend_back(own, base, qkv, probs, ctx, dctx, x, w, dlow, sums1, sums2, given=None):
    cols, seg = ctx.shape
    d = x.shape[1]
    arrays = [qkv, probs, ctx, *dctx, x, w, *dlow, *sums1, *sums2]
    if given is not None:
        arrays.append(given)
    return vmem_call(
        partial(attend_back_kernel, own),
        [((4 * cols + TAIL, d), BF), ((seg, d), F32 if given is None else BF)],
        [base],
        arrays,
        scratch=[pltpu.VMEM((TAIL, d), F32), pltpu.VMEM((3 * cols, seg), BF)],
    )


def grad_kernel(base_ref, dma_ref, dmb_ref, mine_ref, peer_ref, out_ref):
    total = mine_ref[...].astype(F32) + peer_ref[...].astype(F32)
    out_ref[0:HALF] = (dma_ref[...] + total[0:HALF]).astype(BF)
    out_ref[HALF:] = (dmb_ref[...] + total[HALF:]).astype(BF)


def place_kernel(base_ref, *refs):
    out_ref = refs[-1]
    each = len(refs) // 2
    own = pl.multiple_of(base_ref[0], SEG)
    other = pl.multiple_of(SEG - base_ref[0], SEG)
    at = 0
    for mine_ref, came_ref in zip(refs[:each], refs[each:-1]):
        rows = mine_ref.shape[0]
        out_ref[pl.ds(own + at, rows), :] = mine_ref[...]
        out_ref[pl.ds(other + at, rows), :] = came_ref[...]
        at += rows


def place(base, own, came):
    return vmem_call(
        place_kernel, [((2 * SEG, own[0].shape[1]), BF)], [base], [*own, *came]
    )[0]


X, Z0, Z1 = range(3)


def hop(array, size, bit):
    return lax.ppermute(array, "dp", [(i, i ^ (1 << bit)) for i in range(size)])


def add_kernel(bit_ref, mine_ref, came_ref, *refs):
    total = mine_ref[...].astype(F32) + came_ref[...].astype(F32)
    if len(refs) == 1:
        refs[0][...] = total.astype(BF)
        return
    keep_ref, send_ref, total_ref = refs
    rows = keep_ref.shape[0]
    total_ref[...] = total.astype(BF)
    keep_ref[...] = total_ref[pl.ds(pl.multiple_of(bit_ref[0] * rows, 8), rows), :]
    send_ref[...] = total_ref[pl.ds(pl.multiple_of((1 - bit_ref[0]) * rows, 8), rows), :]


def add(bit, mine, came, halves):
    rows, d = mine.shape
    if not halves:
        return vmem_call(add_kernel, [((rows, d), BF)], [bit], [mine, came], limit=8)[0]
    return vmem_call(
        add_kernel, [((rows // 2, d), BF)] * 2, [bit], [mine, came], limit=8,
        scratch=[pltpu.VMEM((rows, d), BF)],
    )


def join_kernel(spans, bit_ref, mine_ref, came_ref, *refs):
    both_ref = refs[-1] if len(refs) > len(spans) else refs[0]
    rows = mine_ref.shape[0]
    own = pl.multiple_of(bit_ref[0] * rows, 8)
    other = pl.multiple_of((1 - bit_ref[0]) * rows, 8)
    both_ref[pl.ds(own, rows), :] = mine_ref[...].astype(both_ref.dtype)
    both_ref[pl.ds(other, rows), :] = came_ref[...].astype(both_ref.dtype)
    if len(refs) > len(spans):
        at = 0
        for ref, span in zip(refs, spans):
            ref[...] = both_ref[at : at + span, :].astype(ref.dtype)
            at += span


def join(bit, mine, came, spans, dtype):
    rows, d = mine.shape
    scratch = [] if len(spans) == 1 else [pltpu.VMEM((2 * rows, d), BF)]
    return vmem_call(
        partial(join_kernel, spans), [((span, d), dtype) for span in spans], [bit], [mine, came],
        limit=8, scratch=scratch,
    )


class Line:
    def __init__(self):
        self.last = None

    def at(self, value):
        return value if self.last is None else after(value, self.last)

    def done(self, value):
        self.last = value
        return value


def reduce_dp(line, mine, came, size, spans, order=(X, Z0, Z1)):
    if size != 8:
        rows = mine.shape[0]
        total = lax.psum((mine.astype(F32) + came.astype(F32)).astype(BF), "dp").astype(F32)
        for _ in range(6):
            yield None
        ends = [sum(spans[: k + 1]) for k in range(len(spans))]
        yield [total[e - n : e] for e, n in zip(ends, spans)]
        return
    place_in = lax.axis_index("dp")
    bits = [jnp.reshape((place_in >> k) & 1, (1,)).astype(jnp.int32) for k in range(3)]
    for bit in order:
        mine, send = add(line.at(bits[bit]), mine, came, True)
        line.done(send)
        came = hop(send, size, bit)
        yield None
    mine = line.done(add(line.at(bits[order[0]]), mine, came, False))
    for bit in order[::-1]:
        came = hop(mine, size, bit)
        yield None
        last = bit == order[0]
        parts = join(line.at(bits[bit]), mine, came, spans if last else (2 * mine.shape[0],),
                     F32 if last else BF)
        mine = line.done(parts[0])
    yield parts


def pick_row(k):
    return jnp.asarray(np.eye(8, dtype=bool)[:, k : k + 1])


def shards(dp_size, tensor_size, seg_input, w_qkv, b_qv, w_out, b_out, norm1_gain, norm1_bias,
           w_up, b_up, w_down, b_down, norm2_gain, norm2_bias, doc_ids, mem_live, out_grad):
    d = seg_input.shape[1]
    cols = w_qkv.shape[2]
    place_in = lax.axis_index("tensor")
    core = place_in % 2
    base = jnp.reshape(core * SEG, (1,)).astype(jnp.int32)
    near = [(i, i ^ 1) for i in range(tensor_size)]
    far = [(i, i ^ 2) for i in range(tensor_size)]

    def to_core(a):
        return lax.ppermute(a, "tensor", near)

    def to_peer(a):
        return lax.ppermute(a, "tensor", far)

    spot = jnp.arange(SEG, dtype=jnp.int32)[None]
    token = (spot >= MEM) & (spot < MEM + SEGTOK)
    dead = (spot < MEM) & (spot >= mem_live[:, None])
    padded = jnp.pad(doc_ids, ((0, 0), (MEM, SEG - MEM - SEGTOK)))
    codes = jnp.where(token, padded, jnp.where(dead, -2, -1)).astype(BF)
    bias_o = jnp.where(pick_row(0), b_up, jnp.pad(b_qv, ((1, 5), (0, d - cols))))

    line = Line()

    def now():
        return line.at(base)

    own_input = lax.dynamic_slice_in_dim(seg_input, core * SEG, SEG, 0)

    w_o = jnp.transpose(w_qkv, (1, 2, 0)).reshape(3 * cols, d)
    bias_p = to_core(bias_o)
    w_p = to_core(w_o)
    wout_e = to_peer(w_out)
    up_p = to_core(w_up)

    ctx_o, probs_o, qkv_o = attend(base, codes, own_input, w_o, bias_o, True)
    line.done(ctx_o)
    ctx_eo = to_peer(ctx_o)
    wout_p = to_core(line.at(w_out))
    down_p = to_core(line.at(w_down))
    ups, downs = (w_up, up_p), (w_down, down_p)
    ctx_p, probs_p, qkv_p = attend(after(now(), up_p), codes, own_input, w_p, bias_p, False)
    line.done(ctx_p)
    ctx_ep = to_peer(ctx_p)
    wout_ep = to_core(wout_e)
    vec = jnp.zeros((8, d), BF)
    for k, one in enumerate(line.at((b_out, norm1_gain, norm1_bias, b_down, norm2_gain,
                                     norm2_bias, b_up))):
        vec = jnp.where(pick_row(k), one, vec)
    line.done(vec)
    fwd = []
    for k in range(2):
        fwd.append(ffn(k, now(), (ctx_o, ctx_p, ctx_eo, ctx_ep), (w_out, wout_p, wout_e, wout_ep),
                       own_input, vec, bias_p, ups, downs))
        line.done(fwd[-1][-1])
    xhat, rstd, low, act_o, act_p, dg_o, dg_p, part = zip(*fwd)
    peer = [to_peer(p) for p in part]
    bwd = []
    for k in range(2):
        bwd.append(back(k, now(), part[k], peer[k], xhat[k], vec, out_grad, (dg_o[k], dg_p[k]),
                        ups, downs))
        line.done(bwd[-1][-2])
    out, dsec, dlow, dh_o, dh_p, npart, sums2 = zip(*bwd)
    npeer = [to_peer(p) for p in npart]
    gdown_p = to_core(line.done(wgrad(now(), act_p, dlow)))
    gup_p = to_core(line.done(wgrad(now(), low, dh_p)))
    gdown = line.done(wgrad(now(), act_o, dlow))
    gup = line.done(wgrad(now(), low, dh_o))
    chains = {
        "D": reduce_dp(line, gdown, gdown_p, dp_size, gdown.shape[:1], (Z0, Z1, X)),
        "U": reduce_dp(line, gup, gup_p, dp_size, gup.shape[:1]),
    }
    sums = {}

    def go(names):
        for name in names:
            sums[name] = next(chains[name])

    mixes = []
    for k in range(2):
        mixes.append(mix_back(now(), dsec[k], npart[k], npeer[k], xhat[k], rstd[k], vec,
                              (w_out, wout_p)))
        line.done(mixes[-1][1])
        if k == 0:
            go("DU")
    dmix, dmlow, dc_o, dc_p, sums1 = zip(*mixes)
    gw_p, ipart = attend_back(False, now(), qkv_p, probs_p, ctx_p, dc_p, own_input, w_p, dmlow,
                              sums1, sums2)
    line.done(gw_p)
    gw_p = to_core(gw_p)
    gw_o, ipart = attend_back(True, now(), qkv_o, probs_o, ctx_o, dc_o, own_input, w_o, dmlow,
                              sums1, sums2, ipart)
    line.done(gw_o)
    ipeer = to_peer(ipart)
    chains["R"] = reduce_dp(line, gw_o, gw_p, dp_size, (cols, 3 * cols, TAIL))
    go("UDRUDR")
    own_grad = line.done(vmem_call(grad_kernel, [((SEG, d), BF)], [now()],
                                   [*dmix, ipart, ipeer])[0])
    own_came = to_core(own_grad)
    go("UDRUD")
    grad_input = line.done(place(now(), [own_grad], [own_came]))
    out_came = [to_core(line.at(o)) for o in out]
    go("RURU")
    seg_output = line.done(place(now(), out, out_came))
    go("DRDR")

    (grad_w_down,), (grad_w_up,), (grad_w_out, grad_qkv, tail) = (sums[k] for k in "DUR")

    grad_w_qkv = jnp.transpose(grad_qkv.reshape(3, cols, d), (2, 0, 1))
    grad_b_qv = jnp.stack([tail[B_QV, 0:cols], tail[B_QV, V_AT : V_AT + cols]])
    return (seg_output, grad_input, grad_w_qkv, grad_b_qv, grad_w_out, tail[B_OUT], tail[GAIN1],
            tail[SHIFT1], grad_w_up, tail[B_UP], grad_w_down, tail[B_DOWN], tail[GAIN2],
            tail[SHIFT2])


def solution(mesh):
    wide, col, row, one = P("dp", None), P(None, "tensor"), P("tensor", None), P()
    return jax.shard_map(
        partial(shards, mesh.shape["dp"], mesh.shape["tensor"]),
        mesh=mesh,
        in_specs=(wide, P(None, None, "tensor"), col, row, one, one, one, col, P("tensor"), row,
                  one, one, one, wide, P("dp"), wide),
        out_specs=(wide, wide, P(None, None, "tensor"), col, row, one, one, one, col, P("tensor"),
                   row, one, one, one),
        check_vma=False,
    )
```

```python
from functools import partial

import jax
import jax.numpy as jnp
import numpy as np
from jax import lax
from jax.experimental import pallas as pl
from jax.experimental.pallas import tpu as pltpu
from jax.sharding import PartitionSpec as P

HEAD = 64
MEM = 10
SEGTOK = 492
SEG = 512
HALF = 256
MASKED_SCORE = -1e30
NORM_EPS = 1e-05
BF = jnp.bfloat16
F32 = jnp.float32
B_OUT, GAIN1, SHIFT1, B_DOWN, GAIN2, SHIFT2, B_UP, B_QV = range(8)
TAIL = 64
PACE = 10_000_000_000
V_AT = 256


def dot(left, right, left_dim, right_dim):
    return lax.dot_general(
        left, right, (((left_dim,), (right_dim,)), ((), ())), preferred_element_type=F32
    )


def after(value, *earlier):
    return lax.optimization_barrier((value, *earlier))[0]


def vmem_call(body, outs, scalars, arrays, scratch=(), limit=16, pace=PACE, far_outs=()):
    near = pl.BlockSpec(memory_space=pltpu.VMEM)
    return pl.pallas_call(
        body,
        out_shape=[jax.ShapeDtypeStruct(s, d) for s, d in outs]
        + [pltpu.HBM(s, d) for s, d in far_outs],
        in_specs=[pl.BlockSpec(memory_space=pltpu.SMEM)] * len(scalars) + [near] * len(arrays),
        out_specs=[near] * len(outs) + [pl.BlockSpec(memory_space=pltpu.HBM)] * len(far_outs),
        scratch_shapes=list(scratch),
        compiler_params=pltpu.CompilerParams(vmem_limit_bytes=limit << 20),
        cost_estimate=pl.CostEstimate(flops=pace, bytes_accessed=0, transcendentals=0),
    )(*scalars, *arrays)


def attend_kernel(base_ref, codes_ref, x_ref, w_ref, bias_ref, ctx_ref, *refs):
    p_ref, qkv_ref, mask_ref = refs[-4:-1] if len(refs) == 6 else refs
    cols = ctx_ref.shape[0]
    heads = cols // HEAD
    core = base_ref[0] // SEG
    proj = dot(w_ref[...], x_ref[...], 1, 1)
    line = lax.broadcasted_iota(jnp.int32, (8, SEG), 0)
    b_query = dot(bias_ref[:, 0:cols], (line == 1).astype(BF), 0, 0)
    b_value = dot(bias_ref[:, 0:cols], (line == 2).astype(BF), 0, 0)
    qkv_ref[0:cols, :] = (proj[0:cols] + b_query).astype(BF)
    qkv_ref[cols : 2 * cols, :] = proj[cols : 2 * cols].astype(BF)
    qkv_ref[2 * cols :, :] = (proj[2 * cols :] + b_value).astype(BF)
    codes = codes_ref[...].astype(F32)
    key_line = jnp.where(core == 0, codes[0:1], codes[1:2])
    spot = lax.broadcasted_iota(jnp.int32, (1, SEG), 1)
    token = (spot >= MEM) & (spot < MEM + SEGTOK)
    query_code = jnp.where(token, key_line, 99.0)
    first = (lax.broadcasted_iota(jnp.int32, (16, SEG), 0) == 0).astype(BF)
    key_code = dot(jnp.broadcast_to(key_line, (16, SEG)).astype(BF), first, 0, 0)
    allowed = (key_code == query_code) | (key_code == -1.0)
    allowed = allowed | ((query_code == 99.0) & (key_code >= 0.0))
    mask_ref[...] = jnp.where(allowed, 0.0, MASKED_SCORE)
    for h in range(heads):
        at = h * HEAD
        query = qkv_ref[at : at + HEAD, :] * BF(HEAD**-0.5)
        key = qkv_ref[cols + at : cols + at + HEAD, :]
        value = qkv_ref[2 * cols + at : 2 * cols + at + HEAD, :]
        scores = dot(key, query, 0, 0) + mask_ref[...]
        top = jnp.max(scores, axis=0, keepdims=True)
        exps = jnp.exp(scores - top)
        total = jnp.sum(exps, axis=0, keepdims=True)
        probs = (exps * (1.0 / total)).astype(BF)
        p_ref[h] = probs
        ctx_ref[at : at + HEAD, :] = dot(value, probs, 1, 0).astype(BF)
    if len(refs) == 6:
        sems = refs[-1]
        copies = [pltpu.make_async_copy(p_ref, refs[0], sems.at[0]),
                  pltpu.make_async_copy(qkv_ref, refs[1], sems.at[1])]
        for copy in copies:
            copy.start()
        for copy in copies:
            copy.wait()


def attend(base, codes, x, w, bias, far):
    cols = w.shape[0] // 3
    heads = cols // HEAD
    saved = [((heads, SEG, SEG), BF), ((3 * cols, SEG), BF)]
    scratch = [pltpu.VMEM((SEG, SEG), F32)]
    if far:
        scratch = [pltpu.VMEM(*one) for one in saved] + scratch + [pltpu.SemaphoreType.DMA((2,))]
    return vmem_call(
        attend_kernel,
        [((cols, SEG), BF)] + ([] if far else saved),
        [base],
        [codes, x, w, bias],
        scratch=scratch,
        far_outs=saved if far else (),
    )


def ffn_kernel(
    chunk,
    base_ref,
    co_ref, cp_ref, eo_ref, ep_ref,
    wo_ref, wp_ref, wye_ref, wyp_ref,
    x_ref, veco_ref, vecp_ref,
    upo_ref, upp_ref, dno_ref, dnp_ref,
    xhat_ref, rstd_ref, low_ref, acto_ref, actp_ref, dgo_ref, dgp_ref, part_ref,
):
    span = slice(chunk * HALF, (chunk + 1) * HALF)
    mine = dot(co_ref[:, span], wo_ref[...], 0, 0) + dot(cp_ref[:, span], wp_ref[...], 0, 0)
    peer = dot(eo_ref[:, span], wye_ref[...], 0, 0) + dot(ep_ref[:, span], wyp_ref[...], 0, 0)
    attn = mine.astype(BF).astype(F32) + peer.astype(BF).astype(F32)
    vec = veco_ref[...].astype(F32)
    mixed = x_ref[span, :].astype(F32) + attn + vec[B_OUT : B_OUT + 1]
    mean = jnp.mean(mixed, axis=-1, keepdims=True)
    centred = mixed - mean
    rstd = lax.rsqrt(jnp.mean(centred * centred, axis=-1, keepdims=True) + NORM_EPS)
    xhat = centred * rstd
    xhat_ref[...] = xhat
    rstd_ref[...] = rstd
    low = (xhat * vec[GAIN1 : GAIN1 + 1] + vec[SHIFT1 : SHIFT1 + 1]).astype(BF)
    low_ref[...] = low
    down = None
    for up_ref, dn_ref, bias, act_ref, dg_ref in (
        (upo_ref, dno_ref, vec[B_UP : B_UP + 1], acto_ref, dgo_ref),
        (upp_ref, dnp_ref, vecp_ref[...].astype(F32)[0:1], actp_ref, dgp_ref),
    ):
        hidden = dot(low, up_ref[...], 1, 0) + bias
        phi = 0.5 + 0.5 * lax.erf(hidden * (0.5**0.5))
        dens = jnp.exp(hidden * hidden * -0.5) * (0.5 * 2.0**0.5 / jnp.pi**0.5)
        act = (hidden * phi).astype(BF)
        act_ref[...] = act
        dg_ref[...] = (phi + hidden * dens).astype(BF)
        term = dot(act, dn_ref[...], 1, 0)
        down = term if down is None else down + term
    part_ref[...] = down.astype(BF)


def ffn(chunk, base, ctxs, wouts, x, veco, vecp, ups, downs):
    d = x.shape[1]
    f = ups[0].shape[1]
    rows = HALF
    return vmem_call(
        partial(ffn_kernel, chunk),
        [((rows, d), F32), ((rows, 1), F32), ((rows, d), BF)]
        + [((rows, f), BF)] * 4
        + [((rows, d), BF)],
        [base],
        [*ctxs, *wouts, x, veco, vecp, *ups, *downs],
    )


def back_kernel(
    chunk,
    base_ref,
    mine_ref, peer_ref, xhat_ref, vec_ref, grad_ref,
    dgo_ref, dgp_ref, upo_ref, upp_ref, dno_ref, dnp_ref,
    out_ref, dsec_ref, dlow_ref, dho_ref, dhp_ref, part_ref, sums_ref,
):
    base = pl.multiple_of(base_ref[0] + chunk * HALF, HALF)
    vec = vec_ref[...].astype(F32)
    normed = xhat_ref[...] * vec[GAIN1 : GAIN1 + 1] + vec[SHIFT1 : SHIFT1 + 1]
    total = mine_ref[...].astype(F32) + peer_ref[...].astype(F32)
    second = normed + total + vec[B_DOWN : B_DOWN + 1]
    mean = jnp.mean(second, axis=-1, keepdims=True)
    centred = second - mean
    rstd = lax.rsqrt(jnp.mean(centred * centred, axis=-1, keepdims=True) + NORM_EPS)
    xhat = centred * rstd
    gain = vec[GAIN2 : GAIN2 + 1]
    out_ref[...] = (xhat * gain + vec[SHIFT2 : SHIFT2 + 1]).astype(BF)
    grad = grad_ref[pl.ds(base, HALF), :].astype(F32)
    scaled = grad * gain
    dsec = rstd * (
        scaled
        - jnp.mean(scaled, axis=-1, keepdims=True)
        - xhat * jnp.mean(scaled * xhat, axis=-1, keepdims=True)
    )
    dsec_ref[...] = dsec
    dlow = dsec.astype(BF)
    dlow_ref[...] = dlow
    sums_ref[...] = jnp.zeros_like(sums_ref)
    sums_ref[0:1] = jnp.sum(grad * xhat, axis=0, keepdims=True)
    sums_ref[1:2] = jnp.sum(grad, axis=0, keepdims=True)
    sums_ref[2:3] = jnp.sum(dsec, axis=0, keepdims=True)
    part = None
    for k, (up_ref, dn_ref, dg_ref, dh_ref) in enumerate(
        ((upo_ref, dno_ref, dgo_ref, dho_ref), (upp_ref, dnp_ref, dgp_ref, dhp_ref))
    ):
        dh = dot(dlow, dn_ref[...], 1, 1) * dg_ref[...].astype(F32)
        sums_ref[3 + k : 4 + k] = jnp.sum(dh, axis=0, keepdims=True)
        dh = dh.astype(BF)
        dh_ref[...] = dh
        term = dot(dh, up_ref[...], 1, 1)
        part = term if part is None else part + term
    part_ref[...] = part.astype(BF)


def back(chunk, base, mine, peer, xhat, vec, grad, dgs, ups, downs):
    rows, d = xhat.shape
    f = ups[0].shape[1]
    return vmem_call(
        partial(back_kernel, chunk),
        [((rows, d), BF), ((rows, d), F32), ((rows, d), BF), ((rows, f), BF), ((rows, f), BF)]
        + [((rows, d), BF), ((8, d), F32)],
        [base],
        [mine, peer, xhat, vec, grad, *dgs, *ups, *downs],
        pace=PACE // (1 + 9 * chunk),
    )


def wgrad_kernel(base_ref, la_ref, lb_ref, ra_ref, rb_ref, out_ref):
    total = dot(la_ref[...], ra_ref[...], 0, 0) + dot(lb_ref[...], rb_ref[...], 0, 0)
    out_ref[...] = total.astype(BF)


def wgrad(base, lefts, rights):
    rows, a = lefts[0].shape
    b = rights[0].shape[1]
    return vmem_call(
        wgrad_kernel, [((a, b), BF)], [base], [*lefts, *rights]
    )[0]


def mix_kernel(
    base_ref,
    dsec_ref, mine_ref, peer_ref, xhat_ref, rstd_ref, vec_ref, wo_ref, wp_ref,
    dmix_ref, dlow_ref, dco_ref, dcp_ref, sums_ref,
):
    gain = vec_ref[GAIN1 : GAIN1 + 1].astype(F32)
    grad = mine_ref[...].astype(F32) + peer_ref[...].astype(F32) + dsec_ref[...]
    xhat = xhat_ref[...]
    scaled = grad * gain
    dmix = rstd_ref[...] * (
        scaled
        - jnp.mean(scaled, axis=-1, keepdims=True)
        - xhat * jnp.mean(scaled * xhat, axis=-1, keepdims=True)
    )
    dmix_ref[...] = dmix
    low = dmix.astype(BF)
    dlow_ref[...] = low
    sums_ref[...] = jnp.zeros_like(sums_ref)
    sums_ref[0:1] = jnp.sum(grad * xhat, axis=0, keepdims=True)
    sums_ref[1:2] = jnp.sum(grad, axis=0, keepdims=True)
    sums_ref[2:3] = jnp.sum(dmix, axis=0, keepdims=True)
    dco_ref[...] = dot(wo_ref[...], low, 1, 1).astype(BF)
    dcp_ref[...] = dot(wp_ref[...], low, 1, 1).astype(BF)


def mix_back(base, dsec, mine, peer, xhat, rstd, vec, wouts):
    rows, d = xhat.shape
    cols = wouts[0].shape[0]
    return vmem_call(
        mix_kernel,
        [((rows, d), F32), ((rows, d), BF), ((cols, rows), BF), ((cols, rows), BF), ((8, d), F32)],
        [base],
        [dsec, mine, peer, xhat, rstd, vec, *wouts],
    )


def attend_back_kernel(
    own,
    base_ref,
    qkv_ref, p_ref, ctx_ref, dca_ref, dcb_ref, x_ref, w_ref, dla_ref, dlb_ref,
    s1a_ref, s1b_ref, s2a_ref, s2b_ref, *rest
):
    given_ref = rest[0] if len(rest) == 5 else None
    gw_ref, part_ref, tail_ref, d_ref = rest[-4:]
    cols = ctx_ref.shape[0]
    for h in range(cols // HEAD):
        at = h * HEAD
        query = qkv_ref[at : at + HEAD, :]
        key = qkv_ref[cols + at : cols + at + HEAD, :]
        value = qkv_ref[2 * cols + at : 2 * cols + at + HEAD, :]
        d_ctx = jnp.concatenate([dca_ref[at : at + HEAD, :], dcb_ref[at : at + HEAD, :]], axis=1)
        probs = p_ref[h]
        inner = jnp.sum(
            d_ctx.astype(F32) * ctx_ref[at : at + HEAD, :].astype(F32), axis=0, keepdims=True
        )
        d_probs = dot(value, d_ctx, 0, 0)
        d_scores = (probs.astype(F32) * (d_probs - inner)).astype(BF)
        scale = HEAD**-0.5
        d_ref[at : at + HEAD, :] = (dot(key, d_scores, 1, 0) * scale).astype(BF)
        d_ref[cols + at : cols + at + HEAD, :] = (dot(query, d_scores, 1, 1) * scale).astype(BF)
        d_ref[2 * cols + at : 2 * cols + at + HEAD, :] = dot(d_ctx, probs, 1, 1).astype(BF)
    part = dot(d_ref[...], w_ref[...], 0, 0)
    if given_ref is None:
        part_ref[...] = part
    else:
        part_ref[...] = (part + given_ref[...]).astype(BF)
    gw_ref[0:cols, :] = (
        dot(ctx_ref[:, 0:HALF], dla_ref[...], 1, 0) + dot(ctx_ref[:, HALF:], dlb_ref[...], 1, 0)
    ).astype(BF)
    gw_ref[cols : 4 * cols, :] = dot(d_ref[...], x_ref[...], 1, 0).astype(BF)
    ones = jnp.ones((16, SEG), BF)
    tail_ref[...] = jnp.zeros_like(tail_ref)
    s1 = s1a_ref[...] + s1b_ref[...]
    s2 = s2a_ref[...] + s2b_ref[...]
    tail_ref[B_OUT : B_OUT + 1] = s1[2:3]
    tail_ref[GAIN1 : SHIFT1 + 1] = s1[0:2]
    tail_ref[B_DOWN : B_DOWN + 1] = s2[2:3]
    tail_ref[GAIN2 : SHIFT2 + 1] = s2[0:2]
    tail_ref[B_UP : B_UP + 1] = s2[3:4] if own else s2[4:5]
    tail_ref[B_QV : B_QV + 1, 0:cols] = dot(ones, d_ref[0:cols, :], 1, 1)[0:1]
    tail_ref[B_QV : B_QV + 1, V_AT : V_AT + cols] = dot(ones, d_ref[2 * cols :, :], 1, 1)[0:1]
    gw_ref[4 * cols :, :] = tail_ref[...].astype(BF)


def attend_back(own, base, qkv, probs, ctx, dctx, x, w, dlow, sums1, sums2, given=None):
    cols, seg = ctx.shape
    d = x.shape[1]
    arrays = [qkv, probs, ctx, *dctx, x, w, *dlow, *sums1, *sums2]
    if given is not None:
        arrays.append(given)
    return vmem_call(
        partial(attend_back_kernel, own),
        [((4 * cols + TAIL, d), BF), ((seg, d), F32 if given is None else BF)],
        [base],
        arrays,
        scratch=[pltpu.VMEM((TAIL, d), F32), pltpu.VMEM((3 * cols, seg), BF)],
    )


def grad_kernel(base_ref, dma_ref, dmb_ref, mine_ref, peer_ref, out_ref):
    total = mine_ref[...].astype(F32) + peer_ref[...].astype(F32)
    out_ref[0:HALF] = (dma_ref[...] + total[0:HALF]).astype(BF)
    out_ref[HALF:] = (dmb_ref[...] + total[HALF:]).astype(BF)


def place_kernel(base_ref, *refs):
    out_ref = refs[-1]
    each = len(refs) // 2
    own = pl.multiple_of(base_ref[0], SEG)
    other = pl.multiple_of(SEG - base_ref[0], SEG)
    at = 0
    for mine_ref, came_ref in zip(refs[:each], refs[each:-1]):
        rows = mine_ref.shape[0]
        out_ref[pl.ds(own + at, rows), :] = mine_ref[...]
        out_ref[pl.ds(other + at, rows), :] = came_ref[...]
        at += rows


def place(base, own, came):
    return vmem_call(
        place_kernel, [((2 * SEG, own[0].shape[1]), BF)], [base], [*own, *came]
    )[0]


X, Z0, Z1 = range(3)


def hop(array, size, bit):
    return lax.ppermute(array, "dp", [(i, i ^ (1 << bit)) for i in range(size)])


def add_kernel(bit_ref, mine_ref, came_ref, *refs):
    total = mine_ref[...].astype(F32) + came_ref[...].astype(F32)
    if len(refs) == 1:
        refs[0][...] = total.astype(BF)
        return
    keep_ref, send_ref, total_ref = refs
    rows = keep_ref.shape[0]
    total_ref[...] = total.astype(BF)
    keep_ref[...] = total_ref[pl.ds(pl.multiple_of(bit_ref[0] * rows, 8), rows), :]
    send_ref[...] = total_ref[pl.ds(pl.multiple_of((1 - bit_ref[0]) * rows, 8), rows), :]


def add(bit, mine, came, halves):
    rows, d = mine.shape
    if not halves:
        return vmem_call(add_kernel, [((rows, d), BF)], [bit], [mine, came], limit=8)[0]
    return vmem_call(
        add_kernel, [((rows // 2, d), BF)] * 2, [bit], [mine, came], limit=8,
        scratch=[pltpu.VMEM((rows, d), BF)],
    )


def join_kernel(spans, bit_ref, mine_ref, came_ref, *refs):
    both_ref = refs[-1] if len(refs) > len(spans) else refs[0]
    rows = mine_ref.shape[0]
    own = pl.multiple_of(bit_ref[0] * rows, 8)
    other = pl.multiple_of((1 - bit_ref[0]) * rows, 8)
    both_ref[pl.ds(own, rows), :] = mine_ref[...].astype(both_ref.dtype)
    both_ref[pl.ds(other, rows), :] = came_ref[...].astype(both_ref.dtype)
    if len(refs) > len(spans):
        at = 0
        for ref, span in zip(refs, spans):
            ref[...] = both_ref[at : at + span, :].astype(ref.dtype)
            at += span


def join(bit, mine, came, spans, dtype):
    rows, d = mine.shape
    scratch = [] if len(spans) == 1 else [pltpu.VMEM((2 * rows, d), BF)]
    return vmem_call(
        partial(join_kernel, spans), [((span, d), dtype) for span in spans], [bit], [mine, came],
        limit=8, scratch=scratch,
    )


class Line:
    def __init__(self):
        self.last = None

    def at(self, value):
        return value if self.last is None else after(value, self.last)

    def done(self, value):
        self.last = value
        return value


def reduce_dp(line, mine, came, size, spans, order=(X, Z0, Z1)):
    if size != 8:
        rows = mine.shape[0]
        total = lax.psum((mine.astype(F32) + came.astype(F32)).astype(BF), "dp").astype(F32)
        for _ in range(6):
            yield None
        ends = [sum(spans[: k + 1]) for k in range(len(spans))]
        yield [total[e - n : e] for e, n in zip(ends, spans)]
        return
    place_in = lax.axis_index("dp")
    bits = [jnp.reshape((place_in >> k) & 1, (1,)).astype(jnp.int32) for k in range(3)]
    for bit in order:
        mine, send = add(line.at(bits[bit]), mine, came, True)
        line.done(send)
        came = hop(send, size, bit)
        yield None
    mine = line.done(add(line.at(bits[order[0]]), mine, came, False))
    for bit in order[::-1]:
        came = hop(mine, size, bit)
        yield None
        last = bit == order[0]
        parts = join(line.at(bits[bit]), mine, came, spans if last else (2 * mine.shape[0],),
                     F32 if last else BF)
        mine = line.done(parts[0])
    yield parts


def pick_row(k):
    return jnp.asarray(np.eye(8, dtype=bool)[:, k : k + 1])


def shards(dp_size, tensor_size, seg_input, w_qkv, b_qv, w_out, b_out, norm1_gain, norm1_bias,
           w_up, b_up, w_down, b_down, norm2_gain, norm2_bias, doc_ids, mem_live, out_grad):
    d = seg_input.shape[1]
    cols = w_qkv.shape[2]
    place_in = lax.axis_index("tensor")
    core = place_in % 2
    base = jnp.reshape(core * SEG, (1,)).astype(jnp.int32)
    near = [(i, i ^ 1) for i in range(tensor_size)]
    far = [(i, i ^ 2) for i in range(tensor_size)]

    def to_core(a):
        return lax.ppermute(a, "tensor", near)

    def to_peer(a):
        return lax.ppermute(a, "tensor", far)

    spot = jnp.arange(SEG, dtype=jnp.int32)[None]
    token = (spot >= MEM) & (spot < MEM + SEGTOK)
    dead = (spot < MEM) & (spot >= mem_live[:, None])
    padded = jnp.pad(doc_ids, ((0, 0), (MEM, SEG - MEM - SEGTOK)))
    codes = jnp.where(token, padded, jnp.where(dead, -2, -1)).astype(BF)
    bias_o = jnp.where(pick_row(0), b_up, jnp.pad(b_qv, ((1, 5), (0, d - cols))))

    line = Line()

    def now():
        return line.at(base)

    own_input = lax.dynamic_slice_in_dim(seg_input, core * SEG, SEG, 0)

    w_o = jnp.transpose(w_qkv, (1, 2, 0)).reshape(3 * cols, d)
    bias_p = to_core(bias_o)
    w_p = to_core(w_o)
    wout_e = to_peer(w_out)
    up_p = to_core(w_up)

    ctx_o, probs_o, qkv_o = attend(base, codes, own_input, w_o, bias_o, True)
    line.done(ctx_o)
    ctx_eo = to_peer(ctx_o)
    wout_p = to_core(line.at(w_out))
    down_p = to_core(line.at(w_down))
    ups, downs = (w_up, up_p), (w_down, down_p)
    ctx_p, probs_p, qkv_p = attend(after(now(), up_p), codes, own_input, w_p, bias_p, False)
    line.done(ctx_p)
    ctx_ep = to_peer(ctx_p)
    wout_ep = to_core(wout_e)
    vec = jnp.zeros((8, d), BF)
    for k, one in enumerate(line.at((b_out, norm1_gain, norm1_bias, b_down, norm2_gain,
                                     norm2_bias, b_up))):
        vec = jnp.where(pick_row(k), one, vec)
    line.done(vec)
    fwd = []
    for k in range(2):
        fwd.append(ffn(k, now(), (ctx_o, ctx_p, ctx_eo, ctx_ep), (w_out, wout_p, wout_e, wout_ep),
                       own_input, vec, bias_p, ups, downs))
        line.done(fwd[-1][-1])
    xhat, rstd, low, act_o, act_p, dg_o, dg_p, part = zip(*fwd)
    peer = [to_peer(p) for p in part]
    bwd = []
    for k in range(2):
        bwd.append(back(k, now(), part[k], peer[k], xhat[k], vec, out_grad, (dg_o[k], dg_p[k]),
                        ups, downs))
        line.done(bwd[-1][-2])
    out, dsec, dlow, dh_o, dh_p, npart, sums2 = zip(*bwd)
    npeer = [to_peer(p) for p in npart]
    gdown_p = to_core(line.done(wgrad(now(), act_p, dlow)))
    gup_p = to_core(line.done(wgrad(now(), low, dh_p)))
    gdown = line.done(wgrad(now(), act_o, dlow))
    gup = line.done(wgrad(now(), low, dh_o))
    chains = {
        "D": reduce_dp(line, gdown, gdown_p, dp_size, gdown.shape[:1], (Z0, Z1, X)),
        "U": reduce_dp(line, gup, gup_p, dp_size, gup.shape[:1]),
    }
    sums = {}

    def go(names):
        for name in names:
            sums[name] = next(chains[name])

    mixes = []
    for k in range(2):
        mixes.append(mix_back(now(), dsec[k], npart[k], npeer[k], xhat[k], rstd[k], vec,
                              (w_out, wout_p)))
        line.done(mixes[-1][1])
        if k == 0:
            go("DU")
    dmix, dmlow, dc_o, dc_p, sums1 = zip(*mixes)
    gw_p, ipart = attend_back(False, now(), qkv_p, probs_p, ctx_p, dc_p, own_input, w_p, dmlow,
                              sums1, sums2)
    line.done(gw_p)
    gw_p = to_core(gw_p)
    gw_o, ipart = attend_back(True, now(), qkv_o, probs_o, ctx_o, dc_o, own_input, w_o, dmlow,
                              sums1, sums2, ipart)
    line.done(gw_o)
    ipeer = to_peer(ipart)
    chains["R"] = reduce_dp(line, gw_o, gw_p, dp_size, (cols, 3 * cols, TAIL))
    go("UDRUDR")
    own_grad = line.done(vmem_call(grad_kernel, [((SEG, d), BF)], [now()],
                                   [*dmix, ipart, ipeer])[0])
    own_came = to_core(own_grad)
    go("UDRU")
    grad_input = line.done(place(now(), [own_grad], [own_came]))
    go("DR")
    out_came = [to_core(line.at(o)) for o in out]
    go("URD")
    seg_output = line.done(place(now(), out, out_came))
    go("URDR")

    (grad_w_down,), (grad_w_up,), (grad_w_out, grad_qkv, tail) = (sums[k] for k in "DUR")

    grad_w_qkv = jnp.transpose(grad_qkv.reshape(3, cols, d), (2, 0, 1))
    grad_b_qv = jnp.stack([tail[B_QV, 0:cols], tail[B_QV, V_AT : V_AT + cols]])
    return (seg_output, grad_input, grad_w_qkv, grad_b_qv, grad_w_out, tail[B_OUT], tail[GAIN1],
            tail[SHIFT1], grad_w_up, tail[B_UP], grad_w_down, tail[B_DOWN], tail[GAIN2],
            tail[SHIFT2])


def solution(mesh):
    wide, col, row, one = P("dp", None), P(None, "tensor"), P("tensor", None), P()
    return jax.shard_map(
        partial(shards, mesh.shape["dp"], mesh.shape["tensor"]),
        mesh=mesh,
        in_specs=(wide, P(None, None, "tensor"), col, row, one, one, one, col, P("tensor"), row,
                  one, one, one, wide, P("dp"), wide),
        out_specs=(wide, wide, P(None, None, "tensor"), col, row, one, one, one, col, P("tensor"),
                   row, one, one, one),
        check_vma=False,
    )
```
